32 devices in a mesh: wide: 8 (over y, x, core), narrow: 4 (over z).
Axes of the slice: x: 2, y: 2, z: 4, core: 2. Of those that a mesh axis runs over, the one named last changes fastest.
Arguments:
- features: bfloat16 [131072, 512], P(('wide', 'narrow')), may hold values from -6 to 6
- adjacency: bfloat16 [3072, 128, 128], P(('wide', 'narrow')), may hold values from -0.375 to 0.375
- block_rows: int32 [32, 96], P(('wide', 'narrow')), may hold values from 0 to 31, as said below
- block_cols: int32 [32, 96], P(('wide', 'narrow')), may hold values from 0 to 39, as said below
- block_count: int32 [32], P(('wide', 'narrow')), may hold values from 40 to 96, as said below
- node_count: int32 [32], P(('wide', 'narrow')), may hold values from 2048 to 4096, as said below
- halo_index: int32 [32, 4, 256], P(('wide', 'narrow')), may hold values from 0 to 2047, as said below
- weight: bfloat16 [512, 512], replicated, may hold values from -0.25 to 0.25
- bias: float32 [512], replicated, may hold values from -3 to 3
- out_grad: bfloat16 [131072, 512], P(('wide', 'narrow')), may hold values from -6 to 6
Outputs:
- output: bfloat16 [131072, 512], P(('wide', 'narrow'))
- input_grad: bfloat16 [131072, 512], P(('wide', 'narrow'))
- weight_grad: float32 [512, 512], replicated
- bias_grad: float32 [512], replicated
The draws below stay inside these ranges and needn't reach their ends.
Inputs may be any that keep to these rules, and one draw needn't show every extreme that they name: `block_count`: each device's live slots include every one of its 32 diagonal blocks and every one of its 8 halo column blocks at least once; some device has all 96 slots live. `block_rows`: within range for live and non-live slots. `block_cols`: within range for live and non-live slots. `node_count`: some device has all 4096 slots live. `halo_index`: the 1024 rows of one device are distinct and all live.
All inputs are finite; a program needn't handle non-finite values.
Results may differ from the reference program's by a relative error of at most 0.0062.
Values may be sent and summed in bfloat16 or wider, within the bound.
A program may use at most 192 MiB of HBM per device.

```python
import math
import jax
import jax.numpy as jnp
from jax import lax

F = 512
BS = 128
NODE_DEV = 4096
HALO = 256
RB = 32
ECB = 40
BLK = 96
TOTAL = 131072
N_WIDE = 8
N_NARROW = 4
DEVICES = 32


def layout_tables(key):
    key_count = jax.random.fold_in(key, 11)
    key_hot = jax.random.fold_in(key, 12)
    key_cold = jax.random.fold_in(key, 13)
    key_rows = jax.random.fold_in(key, 14)
    key_extra = jax.random.fold_in(key, 15)
    key_perm = jax.random.fold_in(key, 16)
    spare = BLK - ECB
    draws = jax.random.randint(key_count, (DEVICES,), 0, spare + 1)
    count = ECB + draws * draws // max(spare, 1)
    hot = jax.random.randint(key_hot, (), 0, DEVICES)
    cold = (hot + 1 + jax.random.randint(key_cold, (), 0, DEVICES - 1)) % DEVICES
    count = count.at[hot].set(BLK).at[cold].set(ECB)
    halo_rowsel = jax.random.randint(key_rows, (DEVICES, ECB - RB), 0, RB)
    fixed_rows = jnp.concatenate([jnp.broadcast_to(jnp.arange(RB, dtype=jnp.int32), (DEVICES, RB)), halo_rowsel.astype(jnp.int32)], 1)
    fixed_cols = jnp.broadcast_to(jnp.arange(ECB, dtype=jnp.int32), (DEVICES, ECB))
    perm_keys = jax.random.split(key_perm, DEVICES)
    perms = jax.vmap(lambda k: jax.random.permutation(k, ECB))(perm_keys)
    fixed_rows = jnp.take_along_axis(fixed_rows, perms, 1)
    fixed_cols = jnp.take_along_axis(fixed_cols, perms, 1)
    extra_rows = jax.random.randint(jax.random.fold_in(key_extra, 1), (DEVICES, spare), 0, RB)
    extra_cols = jax.random.randint(jax.random.fold_in(key_extra, 2), (DEVICES, spare), 0, ECB)
    rows = jnp.concatenate([fixed_rows, extra_rows.astype(jnp.int32)], 1)
    cols = jnp.concatenate([fixed_cols, extra_cols.astype(jnp.int32)], 1)
    return (rows, cols, count.astype(jnp.int32))


def draw_block_rows(key, part):
    return layout_tables(key)[0]


def draw_block_cols(key, part):
    return layout_tables(key)[1]


def draw_block_count(key, part):
    return layout_tables(key)[2]


def draw_node_count(key, part):
    counts = jax.random.randint(jax.random.fold_in(key, 21), (DEVICES,), NODE_DEV // 2, NODE_DEV + 1)
    full = jax.random.randint(jax.random.fold_in(key, 22), (), 0, DEVICES)
    return counts.at[full].set(NODE_DEV).astype(jnp.int32)


def draw_halo_index(key, part):
    keys = jax.random.split(jax.random.fold_in(key, 31), DEVICES)
    picks = jax.vmap(lambda k: jax.random.permutation(k, NODE_DEV // 2)[:4 * HALO])(keys)
    return picks.reshape(DEVICES, 4, HALO).astype(jnp.int32)


def levels(own_key, shape, shards, low, largest):
    def one(axis_at, blocks):
        steps = jax.random.uniform(jax.random.fold_in(jax.random.fold_in(own_key, 6), axis_at), (blocks,), jnp.float32, low / len(shards), largest / len(shards))
        return jnp.repeat(jnp.exp(steps), shape[axis_at] // blocks).reshape((-1,) + (1,) * (len(shape) - axis_at - 1))

    loudness = one(*shards[0])
    for cut in shards[1:]:
        loudness = loudness * one(*cut)
    return loudness


def centred(stream_key, dims, width, bound, pieces=(), kind=jnp.bfloat16):
    values = jax.random.normal(stream_key, dims, jnp.float32) * width
    if len(pieces) > 0:
        values = levels(stream_key, dims, pieces, -0.22, 0.18) * values
    return jnp.clip(values, min=-bound, max=bound).astype(kind)


def setup_inputs(seed: int = 0) -> dict:
    seeds = jax.random.split(jax.random.key(seed), 11)
    features = centred(seeds[0], (TOTAL, F), 1.0, 6.0, ((0, 32),))
    adjacency = centred(seeds[1], (DEVICES * BLK, BS, BS), (2 * BS) ** -0.5, 0.375, ((0, 32),))
    block_rows = draw_block_rows(jax.random.fold_in(seeds[10], 71), 0)
    block_cols = draw_block_cols(jax.random.fold_in(seeds[10], 71), 0)
    block_count = draw_block_count(jax.random.fold_in(seeds[10], 71), 0)
    node_count = draw_node_count(jax.random.fold_in(seeds[10], 71), 0)
    halo_index = draw_halo_index(jax.random.fold_in(seeds[10], 71), 0)
    weight = centred(seeds[7], (F, F), F ** -0.5, 0.25)
    bias = centred(seeds[8], (F,), 0.5, 3.0, (), jnp.float32)
    out_grad = centred(seeds[9], (TOTAL, F), 1.0, 6.0, ((0, 32),))
    return {"features": features, "adjacency": adjacency, "block_rows": block_rows, "block_cols": block_cols, "block_count": block_count, "node_count": node_count, "halo_index": halo_index, "weight": weight, "bias": bias, "out_grad": out_grad}


def device_pass(items, weight, bias):
    own, halos, blocks, rows, cols, count, keep, grads = items
    extended = jnp.concatenate([own, halos], 0).reshape(ECB, BS, F)
    live = jnp.arange(BLK) < count

    def forward_step(total, item):
        tile, row_id, col_id, alive = item
        prod = jnp.dot(tile, extended[col_id], preferred_element_type=jnp.float32)
        return (total.at[row_id].add(jnp.where(alive, prod, jnp.float32(0.0))), None)
    summed, _ = lax.scan(forward_step, jnp.zeros((RB, BS, F), jnp.float32), (blocks, rows, cols, live))
    aggregated = summed.reshape(NODE_DEV, F).astype(jnp.bfloat16)
    pre = jnp.dot(aggregated, weight, preferred_element_type=jnp.float32) + bias
    sig = jax.nn.sigmoid(pre)
    output = jnp.where(keep[:, None], pre * sig, jnp.float32(0.0)).astype(jnp.bfloat16)
    dpre = jnp.where(keep[:, None], grads.astype(jnp.float32) * sig * (1.0 + pre * (1.0 - sig)), jnp.float32(0.0)).astype(jnp.bfloat16)
    weight_part = jnp.dot(aggregated.T, dpre, preferred_element_type=jnp.float32)
    bias_part = lax.optimization_barrier(jnp.sum(dpre.astype(jnp.float32), 0))
    back = jnp.dot(dpre, weight.T, preferred_element_type=jnp.float32).astype(jnp.bfloat16).reshape(RB, BS, F)

    def backward_step(total, item):
        tile, row_id, col_id, alive = item
        prod = jnp.dot(tile.T, back[row_id], preferred_element_type=jnp.float32)
        return (total.at[col_id].add(jnp.where(alive, prod, jnp.float32(0.0))), None)
    spread, _ = lax.scan(backward_step, jnp.zeros((ECB, BS, F), jnp.float32), (blocks, rows, cols, live))
    own_part = spread[:RB].reshape(NODE_DEV, F)
    halo_part = spread[RB:].reshape(4, HALO, F).astype(jnp.bfloat16)
    return (output, weight_part, bias_part, own_part, halo_part)

def reference(features, adjacency, block_rows, block_cols, block_count, node_count, halo_index, weight, bias, out_grad):
    n_wide = N_WIDE
    n_narrow = N_NARROW
    feats = features.reshape(DEVICES, NODE_DEV, F)
    keep = jnp.arange(NODE_DEV)[None, :] < node_count[:, None]
    masked = jnp.where(keep[:, :, None], feats, jnp.zeros_like(feats))
    packed = jax.vmap(lambda rows_of, picks: rows_of[picks])(masked, halo_index)
    grid = packed.reshape(n_wide, n_narrow, 4, HALO, F)
    zero_wide = jnp.zeros((1, n_narrow, HALO, F), jnp.bfloat16)
    zero_narrow = jnp.zeros((n_wide, 1, HALO, F), jnp.bfloat16)
    seg_a = jnp.concatenate([zero_wide, grid[:-1, :, 1]], 0)
    seg_b = jnp.concatenate([grid[1:, :, 0], zero_wide], 0)
    seg_c = jnp.concatenate([zero_narrow, grid[:, :-1, 3]], 1)
    seg_d = jnp.concatenate([grid[:, 1:, 2], zero_narrow], 1)
    halos = jnp.stack([seg_a, seg_b, seg_c, seg_d], 2).reshape(DEVICES, 4 * HALO, F)
    blocks = adjacency.reshape(DEVICES, BLK, BS, BS)
    grads = out_grad.reshape(DEVICES, NODE_DEV, F)
    output, weight_parts, bias_parts, own_part, halo_part = lax.map(lambda items: device_pass(items, weight, bias), (masked, halos, blocks, block_rows, block_cols, block_count, keep, grads))
    scale = 1.0 / math.sqrt(TOTAL)
    weight_grad = lax.optimization_barrier(jnp.sum(weight_parts, 0)) * scale
    bias_grad = lax.optimization_barrier(jnp.sum(bias_parts, 0)) * scale
    hgrid = halo_part.astype(jnp.float32).reshape(n_wide, n_narrow, 4, HALO, F)
    fzero_wide = jnp.zeros((1, n_narrow, HALO, F), jnp.float32)
    fzero_narrow = jnp.zeros((n_wide, 1, HALO, F), jnp.float32)
    in_a = jnp.concatenate([fzero_wide, hgrid[:-1, :, 1]], 0)
    in_b = jnp.concatenate([hgrid[1:, :, 0], fzero_wide], 0)
    in_c = jnp.concatenate([fzero_narrow, hgrid[:, :-1, 3]], 1)
    in_d = jnp.concatenate([hgrid[:, 1:, 2], fzero_narrow], 1)
    incoming = jnp.stack([in_a, in_b, in_c, in_d], 2).reshape(DEVICES, 4 * HALO, F)
    summed = jax.vmap(lambda base, picks, extra: base.at[picks].add(extra))(own_part, halo_index.reshape(DEVICES, 4 * HALO), incoming)
    input_grad = jnp.where(keep[:, :, None], summed, jnp.float32(0.0)).astype(jnp.bfloat16)
    return (output.reshape(TOTAL, F), input_grad.reshape(TOTAL, F), weight_grad, bias_grad)
```

```python
import functools
import math

import jax
import jax.numpy as jnp
from jax import lax
from jax.experimental import pallas as pl
from jax.experimental.pallas import tpu as pltpu
from jax.sharding import PartitionSpec as P

MESH = pl.DeviceIdType.MESH
ANY = pl.ANY
VMEM_LIMIT = 60 * 1024 * 1024


def neighbours(n_wide, n_narrow):
    w = lax.axis_index("wide")
    n = lax.axis_index("narrow")
    return (
        (w > 0, (w - 1, n)),
        (w < n_wide - 1, (w + 1, n)),
        (n > 0, (w, n - 1)),
        (n < n_narrow - 1, (w, n + 1)),
    )


def halo_copy(src, dst, send, recv, k, target):
    return pltpu.make_async_remote_copy(
        src_ref=src.at[k],
        dst_ref=dst.at[k ^ 1],
        send_sem=send.at[k],
        recv_sem=recv.at[k ^ 1],
        device_id=target,
        device_id_type=MESH,
    )


def gather_kernel(n_wide, n_narrow, idx_ref, feat_hbm, halo_ref, feat, packed, load, send, recv):
    count = idx_ref.shape[1]
    span = feat.shape[0]
    fetch = pltpu.make_async_copy(feat_hbm.at[pl.ds(0, span)], feat, load)
    fetch.start()
    near = neighbours(n_wide, n_narrow)
    barrier = pltpu.get_barrier_semaphore()
    for there, target in near:

        @pl.when(there)
        def _():
            pl.semaphore_signal(barrier, inc=1, device_id=target, device_id_type=MESH)

    pl.semaphore_wait(barrier, sum(there.astype(jnp.int32) for there, _ in near))
    fetch.wait()
    lane = lax.broadcasted_iota(jnp.int32, (count, 128), 1).astype(jnp.float32)
    for k in (2, 3, 1, 0):
        there, target = near[k]

        @pl.when(there)
        def _():
            row = idx_ref[pl.ds(k, 1), :].astype(jnp.float32)
            column = jnp.transpose(jnp.broadcast_to(row, (128, count)))
            hot = jnp.concatenate(
                [
                    jnp.where(column == lane + float(at), 1.0, 0.0).astype(jnp.bfloat16)
                    for at in range(0, span, 128)
                ],
                axis=1,
            )
            packed[k] = jnp.dot(hot, feat[...], preferred_element_type=jnp.float32).astype(
                jnp.bfloat16
            )
            halo_copy(packed, halo_ref, send, recv, k, target).start()

        @pl.when(jnp.logical_not(there))
        def _():
            halo_ref[k] = jnp.zeros(halo_ref.shape[1:], halo_ref.dtype)

    for k in range(4):
        there, target = near[k]

        @pl.when(there)
        def _():
            copy = halo_copy(packed, halo_ref, send, recv, k, target)
            copy.wait_send()
            halo_copy(packed, halo_ref, send, recv, k ^ 1, target).wait_recv()


def layer_kernel(
    step,
    rows,
    cols,
    live,
    nodes_live,
    feat_hbm,
    halo_hbm,
    adj_hbm,
    grad_hbm,
    w_ref,
    b_ref,
    out_hbm,
    low_hbm,
    high_hbm,
    ret_hbm,
    wg_ref,
    bg_ref,
    ext,
    adj,
    grad,
    acc,
    back,
    out,
    wsum,
    bsum,
    sem,
    out_sem,
):
    row_blocks, side, width = feat_hbm.shape
    halo_blocks = halo_hbm.shape[0]
    col_blocks = row_blocks + halo_blocks
    low_blocks = low_hbm.shape[0]
    count = live[0]
    keep_to = nodes_live[0]
    loads = [
        pltpu.make_async_copy(feat_hbm, ext.at[pl.ds(0, row_blocks)], sem.at[0]),
        pltpu.make_async_copy(halo_hbm, ext.at[pl.ds(row_blocks, halo_blocks)], sem.at[1]),
        pltpu.make_async_copy(adj_hbm, adj, sem.at[2]),
        pltpu.make_async_copy(grad_hbm, grad, sem.at[3]),
    ]
    for load in loads:
        load.start()

    def clear(i, carry):
        acc[i] = jnp.zeros((side, width), jnp.float32)
        return carry

    lax.fori_loop(0, row_blocks + 1, clear, 0)
    wsum[...] = jnp.zeros_like(wsum)
    bsum[...] = jnp.zeros_like(bsum)
    for load in loads[:3]:
        load.wait()

    def kept(block, blocks=1):
        at = lax.broadcasted_iota(jnp.int32, (blocks * side, width), 0)
        return at < keep_to - block * side

    def mask(i, carry):
        ext[i] = jnp.where(kept(i), ext[i].astype(jnp.float32), 0.0).astype(ext.dtype)
        return carry

    lax.fori_loop(keep_to // side, row_blocks, mask, 0)

    unroll = 4
    trips = (count + unroll - 1) // unroll

    def forward(t, carry):
        for u in range(unroll):
            b = t * unroll + u
            to = jnp.where(b < count, rows[b], row_blocks)
            acc[to] += jnp.dot(adj[b], ext[cols[b]], preferred_element_type=jnp.float32)
        return carry

    lax.fori_loop(0, trips, forward, 0)
    loads[3].wait()

    def put(i):
        return pltpu.make_async_copy(
            out.at[pl.ds(i * step, step)], out_hbm.at[pl.ds(i * step, step)], out_sem.at[i]
        )

    tall = step * side

    def dense(i, carry):
        at = pl.ds(i * step, step)
        agg = acc[at].reshape(tall, width).astype(jnp.bfloat16)
        pre = jnp.dot(agg, w_ref[...], preferred_element_type=jnp.float32) + b_ref[...]
        keep = kept(i * step, step)
        sig = jax.nn.sigmoid(pre)
        res = jnp.where(keep, pre * sig, 0.0).astype(jnp.bfloat16)
        out[at] = res.reshape(step, side, width)
        put(i).start()
        g = grad[at].reshape(tall, width).astype(jnp.float32)
        dpre = jnp.where(keep, g * sig * (1.0 + pre * (1.0 - sig)), 0.0).astype(jnp.bfloat16)
        wsum[...] += lax.dot_general(
            agg, dpre, (((0,), (0,)), ((), ())), preferred_element_type=jnp.float32
        )
        bsum[...] += jnp.sum(dpre.astype(jnp.float32).reshape(tall // 8, 8, width), 0)
        back[at] = (
            lax.dot_general(
                dpre, w_ref[...], (((1,), (1,)), ((), ())), preferred_element_type=jnp.float32
            )
            .astype(jnp.bfloat16)
            .reshape(step, side, width)
        )
        return carry

    lax.fori_loop(0, row_blocks // step, dense, 0)
    wg_ref[...] = wsum[...].astype(wg_ref.dtype)
    bg_ref[...] = jnp.sum(bsum[...], 0, keepdims=True)

    lax.fori_loop(0, col_blocks + 1, clear, 0)

    def backward(t, carry):
        for u in range(unroll):
            b = t * unroll + u
            to = jnp.where(b < count, cols[b], col_blocks)
            acc[to] += lax.dot_general(
                adj[b], back[rows[b]], (((0,), (0,)), ((), ())), preferred_element_type=jnp.float32
            )
        return carry

    lax.fori_loop(0, trips, backward, 0)
    low = pltpu.make_async_copy(acc.at[pl.ds(0, low_blocks)], low_hbm, sem.at[0])
    low.start()

    def narrow_halo(i, carry):
        ext[i] = acc[row_blocks + i].astype(ext.dtype)
        return carry

    lax.fori_loop(0, halo_blocks, narrow_halo, 0)
    ret = pltpu.make_async_copy(ext.at[pl.ds(0, halo_blocks)], ret_hbm, sem.at[1])
    ret.start()

    def narrow_high(i, carry):
        grad[i] = jnp.where(kept(i), acc[i], 0.0).astype(grad.dtype)
        return carry

    lax.fori_loop(low_blocks, row_blocks, narrow_high, 0)
    high = pltpu.make_async_copy(
        grad.at[pl.ds(low_blocks, row_blocks - low_blocks)], high_hbm, sem.at[2]
    )
    high.start()
    low.wait()
    ret.wait()
    high.wait()

    def drain(i, carry):
        put(i).wait()
        return carry

    lax.fori_loop(0, row_blocks // step, drain, 0)


def sum_kernel(
    n_wide,
    n_narrow,
    scale,
    idx_ref,
    keep_ref,
    ret_ref,
    wg_ref,
    bg_ref,
    low_hbm,
    grad_ref,
    wout_ref,
    bout_ref,
    low,
    incoming,
    rs_wide,
    rs_narrow,
    part,
    ag_narrow,
    ag_wide,
    b_wide,
    b_mid,
    b_narrow,
    load,
    send,
    recv,
    send_w,
    recv_w,
    send_n,
    recv_n,
    send_gn,
    recv_gn,
    send_gw,
    recv_gw,
    send_bw,
    recv_bw,
    send_bn,
    recv_bn,
):
    w = lax.axis_index("wide")
    n = lax.axis_index("narrow")
    slab = wg_ref.shape[1]
    part_width = rs_narrow.shape[2]
    fetch = pltpu.make_async_copy(low_hbm, low, load)
    fetch.start()

    def wide_peer(d):
        return (lax.rem(w + d, n_wide), n)

    def narrow_peer(d):
        return (w, lax.rem(n + d, n_narrow))

    peers = [wide_peer(d) for d in range(1, n_wide)] + [
        narrow_peer(d) for d in range(1, n_narrow)
    ]
    barrier = pltpu.get_barrier_semaphore()
    for peer in peers:
        pl.semaphore_signal(barrier, inc=1, device_id=peer, device_id_type=MESH)
    pl.semaphore_wait(barrier, len(peers))

    def remote(src, dst, s, r, peer):
        return pltpu.make_async_remote_copy(
            src_ref=src, dst_ref=dst, send_sem=s, recv_sem=r, device_id=peer, device_id_type=MESH
        )

    pending = []
    near = neighbours(n_wide, n_narrow)

    first = []
    for d in range(1, n_wide):
        peer = wide_peer(d)
        c = remote(wg_ref.at[peer[0]], rs_wide.at[d], send_w.at[d], recv_w.at[d], peer)
        c.start()
        first.append(c)
    bias_first = []
    for d in range(1, n_wide):
        c = remote(bg_ref, b_wide.at[d], send_bw.at[d], recv_bw.at[d], wide_peer(d))
        c.start()
        bias_first.append(c)
    for k in (2, 3, 1, 0):
        there, target = near[k]

        @pl.when(there)
        def _():
            halo_copy(ret_ref, incoming, send, recv, k, target).start()

        @pl.when(jnp.logical_not(there))
        def _():
            incoming[k] = jnp.zeros(incoming.shape[1:], incoming.dtype)

    total = wg_ref[w].astype(jnp.float32)
    for c in first:
        c.wait_recv()
    for d in range(1, n_wide):
        total = total + rs_wide[d].astype(jnp.float32)
    bias = bg_ref[...]
    for c in bias_first:
        c.wait_recv()
    for d in range(1, n_wide):
        bias = bias + b_wide[d]
    b_mid[...] = bias
    for j in range(n_narrow):
        part[j] = total[:, j * part_width : (j + 1) * part_width].astype(part.dtype)
    second = []
    for d in range(1, n_narrow):
        peer = narrow_peer(d)
        c = remote(part.at[peer[1]], rs_narrow.at[d], send_n.at[d], recv_n.at[d], peer)
        c.start()
        second.append(c)
    for d in range(1, n_narrow):
        c = remote(b_mid, b_narrow.at[d], send_bn.at[d], recv_bn.at[d], narrow_peer(d))
        c.start()
        bias_first.append(c)
        second.append(c)
    piece = part[n].astype(jnp.float32)
    for c in second:
        c.wait_recv()
    for d in range(1, n_narrow):
        piece = piece + rs_narrow[d].astype(jnp.float32)
        bias = bias + b_narrow[d]
    bout_ref[...] = bias * scale
    ag_narrow[n] = (piece * scale).astype(ag_narrow.dtype)
    third = []
    for d in range(1, n_narrow):
        c = remote(
            ag_narrow.at[n], ag_narrow.at[n], send_gn.at[d], recv_gn.at[d], narrow_peer(d)
        )
        c.start()
        third.append(c)
    for c in third:
        c.wait_recv()
    fourth = []
    for d in range(1, n_wide):
        c = remote(ag_narrow, ag_wide.at[w], send_gw.at[d], recv_gw.at[d], wide_peer(d))
        c.start()
        fourth.append(c)
    ag_wide[w] = ag_narrow[...]

    for k in range(4):
        there, target = near[k]

        @pl.when(there)
        def _():
            halo_copy(ret_ref, incoming, send, recv, k, target).wait_send()
            halo_copy(ret_ref, incoming, send, recv, k ^ 1, target).wait_recv()

    fetch.wait()
    chunk = low.shape[1]
    merged = incoming[...].reshape(-1, incoming.shape[2])
    idx = idx_ref[...]
    keep_to = keep_ref[...]

    def scatter(i, carry):
        at = lax.broadcasted_iota(jnp.int32, (chunk, idx.shape[1]), 0) + i * chunk
        hot = jnp.where(at == idx, 1.0, 0.0).astype(jnp.bfloat16)
        full = low[i] + jnp.dot(hot, merged, preferred_element_type=jnp.float32)
        row = lax.broadcasted_iota(jnp.int32, full.shape, 0) + i * chunk
        grad_ref[i] = jnp.where(row < keep_to, full, 0.0).astype(grad_ref.dtype)
        return carry

    lax.fori_loop(0, low.shape[0], scatter, 0)
    for c in fourth:
        c.wait_recv()
    for i in range(n_wide):
        for j in range(n_narrow):
            wout_ref[pl.ds(i * slab, slab), pl.ds(j * part_width, part_width)] = ag_wide[
                i, j
            ].astype(jnp.float32)
    for c in first + bias_first + second[: n_narrow - 1] + third + fourth:
        c.wait_send()


def local(
    n_wide,
    n_narrow,
    features,
    adjacency,
    block_rows,
    block_cols,
    block_count,
    node_count,
    halo_index,
    weight,
    bias,
    out_grad,
):
    nodes, width = features.shape
    slots, side, _ = adjacency.shape
    row_blocks = nodes // side
    sides, halo = halo_index.shape[1:]
    halo_blocks = sides * halo // side
    low_blocks = row_blocks // 2
    col_blocks = row_blocks + halo_blocks
    bf, f32 = jnp.bfloat16, jnp.float32
    picks = halo_index[0]
    vm = pl.BlockSpec(memory_space=pltpu.VMEM)
    sm = pl.BlockSpec(memory_space=pltpu.SMEM)
    hb = pl.BlockSpec(memory_space=ANY)
    dma = pltpu.SemaphoreType.DMA

    halos = pl.pallas_call(
        functools.partial(gather_kernel, n_wide, n_narrow),
        name="halo_out",
        out_shape=jax.ShapeDtypeStruct((sides, halo, width), bf),
        in_specs=[vm, hb],
        out_specs=vm,
        scratch_shapes=[
            pltpu.VMEM((nodes // 2, width), bf),
            pltpu.VMEM((sides, halo, width), bf),
            dma,
            dma((sides,)),
            dma((sides,)),
        ],
        compiler_params=pltpu.CompilerParams(
            collective_id=0, has_side_effects=True, vmem_limit_bytes=VMEM_LIMIT
        ),
    )(picks, features)

    step = 2
    blocked = (row_blocks, side, width)
    out, low, high, ret, wg, bg = pl.pallas_call(
        functools.partial(layer_kernel, step),
        name="layer",
        out_shape=(
            jax.ShapeDtypeStruct(blocked, bf),
            jax.ShapeDtypeStruct((low_blocks, side, width), f32),
            jax.ShapeDtypeStruct((row_blocks - low_blocks, side, width), bf),
            jax.ShapeDtypeStruct((halo_blocks, side, width), bf),
            jax.ShapeDtypeStruct((width, width), bf),
            jax.ShapeDtypeStruct((1, width), f32),
        ),
        in_specs=[sm, sm, sm, sm, hb, hb, hb, hb, vm, vm],
        out_specs=(hb, hb, hb, hb, vm, vm),
        scratch_shapes=[
            pltpu.VMEM((col_blocks, side, width), bf),
            pltpu.VMEM((slots, side, side), bf),
            pltpu.VMEM(blocked, bf),
            pltpu.VMEM((col_blocks + 1, side, width), f32),
            pltpu.VMEM(blocked, bf),
            pltpu.VMEM(blocked, bf),
            pltpu.VMEM((width, width), f32),
            pltpu.VMEM((8, width), f32),
            dma((4,)),
            dma((row_blocks // step,)),
        ],
        compiler_params=pltpu.CompilerParams(vmem_limit_bytes=VMEM_LIMIT),
    )(
        block_rows[0],
        block_cols[0],
        block_count,
        node_count,
        features.reshape(blocked),
        halos.reshape(halo_blocks, side, width),
        adjacency,
        out_grad.reshape(blocked),
        weight,
        bias.reshape(1, width),
    )

    slab = width // n_wide
    part_width = width // n_narrow
    scale = 1.0 / math.sqrt(nodes * n_wide * n_narrow)
    chunk = 2 * side
    low_grad, wout, bout = pl.pallas_call(
        functools.partial(sum_kernel, n_wide, n_narrow, scale),
        name="sums",
        out_shape=(
            jax.ShapeDtypeStruct((low_blocks // 2, chunk, width), bf),
            jax.ShapeDtypeStruct((width, width), f32),
            jax.ShapeDtypeStruct((1, width), f32),
        ),
        in_specs=[vm, vm, vm, vm, vm, hb],
        out_specs=(vm, vm, vm),
        scratch_shapes=[
            pltpu.VMEM((low_blocks // 2, chunk, width), f32),
            pltpu.VMEM((sides, halo, width), bf),
            pltpu.VMEM((n_wide, slab, width), bf),
            pltpu.VMEM((n_narrow, slab, part_width), bf),
            pltpu.VMEM((n_narrow, slab, part_width), bf),
            pltpu.VMEM((n_narrow, slab, part_width), bf),
            pltpu.VMEM((n_wide, n_narrow, slab, part_width), bf),
            pltpu.VMEM((n_wide, 1, width), f32),
            pltpu.VMEM((1, width), f32),
            pltpu.VMEM((n_narrow, 1, width), f32),
            dma,
            dma((sides,)),
            dma((sides,)),
        ]
        + [dma((n_wide,))] * 2
        + [dma((n_narrow,))] * 4
        + [dma((n_wide,))] * 4
        + [dma((n_narrow,))] * 2,
        compiler_params=pltpu.CompilerParams(
            collective_id=1, has_side_effects=True, vmem_limit_bytes=VMEM_LIMIT
        ),
    )(
        picks.reshape(1, sides * halo),
        jnp.broadcast_to(node_count.reshape(1, 1), (1, width)),
        ret.reshape(sides, halo, width),
        wg.reshape(n_wide, slab, width),
        bg,
        low.reshape(low_blocks // 2, chunk, width),
    )
    input_grad = jnp.concatenate(
        [low_grad.reshape(-1, width), high.reshape(-1, width)], 0
    )
    return out.reshape(nodes, width), input_grad, wout, bout.reshape(width)


def solution(mesh):
    both = ("wide", "narrow")
    placed = (
        P(both, None),
        P(both, None, None),
        P(both, None),
        P(both, None),
        P(both),
        P(both),
        P(both, None, None),
        P(),
        P(),
        P(both, None),
    )
    return jax.shard_map(
        functools.partial(local, mesh.shape["wide"], mesh.shape["narrow"]),
        mesh=mesh,
        in_specs=placed,
        out_specs=(P(both, None), P(both, None), P(), P()),
        check_vma=False,
    )
```

```python
import functools
import math

import jax
import jax.numpy as jnp
from jax import lax
from jax.experimental import pallas as pl
from jax.experimental.pallas import tpu as pltpu
from jax.sharding import PartitionSpec as P

MESH = pl.DeviceIdType.MESH
ANY = pl.ANY
VMEM_LIMIT = 60 * 1024 * 1024


def neighbours(n_wide, n_narrow):
    w = lax.axis_index("wide")
    n = lax.axis_index("narrow")
    return (
        (w > 0, (w - 1, n)),
        (w < n_wide - 1, (w + 1, n)),
        (n > 0, (w, n - 1)),
        (n < n_narrow - 1, (w, n + 1)),
    )


def halo_copy(src, dst, send, recv, k, target):
    return pltpu.make_async_remote_copy(
        src_ref=src.at[k],
        dst_ref=dst.at[k ^ 1],
        send_sem=send.at[k],
        recv_sem=recv.at[k ^ 1],
        device_id=target,
        device_id_type=MESH,
    )


def tables(row_ref, col_ref, count, row_blocks, col_blocks):
    lanes = row_ref.shape[1]
    f32 = jnp.float32
    lane = lax.broadcasted_iota(jnp.int32, (lanes, lanes), 1).astype(f32)
    sub = lax.broadcasted_iota(jnp.int32, (lanes, lanes), 0).astype(f32)

    def spread(x):
        return jnp.broadcast_to(x.astype(f32), (lanes, lanes))

    halo_blocks = col_blocks - row_blocks
    col = spread(col_ref[...])
    place = jnp.where(col >= row_blocks, col - row_blocks, col + halo_blocks)
    place = jnp.where(lane < spread(count), place, float(col_blocks))
    place_t = jnp.transpose(place)
    row_t = jnp.transpose(spread(row_ref[...]))
    same = place == place_t
    ahead = lane < sub
    one = lambda m: jnp.where(m, 1.0, 0.0)
    rank = jnp.sum(one((place < place_t) | (same & ahead)), 1, keepdims=True)
    twin = jnp.minimum(jnp.sum(one(same & ahead), 1, keepdims=True), 1.0)
    hot = one(jnp.broadcast_to(rank, (lanes, lanes)) == lane)
    pick = lambda x: jnp.sum(hot * x, 0, keepdims=True)
    ends = jnp.sum(one(place_t <= lane), 0, keepdims=True)
    keep = pick(jnp.broadcast_to(twin, (lanes, lanes)))
    return pick(sub), pick(row_t), keep, ends


def gather_kernel(
    n_wide,
    n_narrow,
    row_blocks,
    col_blocks,
    idx_ref,
    row_ref,
    col_ref,
    count_ref,
    feat_hbm,
    halo_ref,
    table_ref,
    feat,
    packed,
    load,
    send,
    recv,
):
    count = idx_ref.shape[1]
    span = feat.shape[0]
    fetch = pltpu.make_async_copy(feat_hbm.at[pl.ds(0, span)], feat, load)
    fetch.start()
    near = neighbours(n_wide, n_narrow)
    barrier = pltpu.get_barrier_semaphore()
    for there, target in near:

        @pl.when(there)
        def _():
            pl.semaphore_signal(barrier, inc=1, device_id=target, device_id_type=MESH)

    fetch.wait()
    lane = lax.broadcasted_iota(jnp.int32, (count, 128), 1).astype(jnp.float32)

    def pack(k):
        row = idx_ref[pl.ds(k, 1), :].astype(jnp.float32)
        column = jnp.transpose(jnp.broadcast_to(row, (128, count)))
        hot = jnp.concatenate(
            [
                jnp.where(column == lane + float(at), 1.0, 0.0).astype(jnp.bfloat16)
                for at in range(0, span, 128)
            ],
            axis=1,
        )
        packed[k] = jnp.dot(hot, feat[...], preferred_element_type=jnp.float32).astype(
            jnp.bfloat16
        )

    pack(2)
    pl.semaphore_wait(barrier, sum(there.astype(jnp.int32) for there, _ in near))
    for k in (2, 3, 1, 0):
        there, target = near[k]
        if k != 2:
            pack(k)

        @pl.when(there)
        def _():
            halo_copy(packed, halo_ref, send, recv, k, target).start()

        @pl.when(jnp.logical_not(there))
        def _():
            halo_ref[k] = jnp.zeros(halo_ref.shape[1:], halo_ref.dtype)

    table_ref[...] = jnp.zeros_like(table_ref)
    for i, line in enumerate(
        tables(row_ref, col_ref, count_ref[...], row_blocks, col_blocks)
    ):
        table_ref[pl.ds(i, 1), :] = line.astype(jnp.int32)

    for k in range(4):
        there, target = near[k]

        @pl.when(there)
        def _():
            halo_copy(packed, halo_ref, send, recv, k, target).wait_send()
            halo_copy(packed, halo_ref, send, recv, k ^ 1, target).wait_recv()


def layer_kernel(
    step,
    rows,
    cols,
    live,
    nodes_live,
    feat_hbm,
    halo_hbm,
    adj_hbm,
    grad_hbm,
    w_ref,
    b_ref,
    out_hbm,
    back_hbm,
    wg_ref,
    bg_ref,
    ext,
    adj,
    grad,
    acc,
    back,
    out,
    wsum,
    bsum,
    sem,
    out_sem,
):
    row_blocks, side, width = feat_hbm.shape
    halo_blocks = halo_hbm.shape[0]
    count = live[0]
    keep_to = nodes_live[0]
    loads = [
        pltpu.make_async_copy(feat_hbm, ext.at[pl.ds(0, row_blocks)], sem.at[0]),
        pltpu.make_async_copy(halo_hbm, ext.at[pl.ds(row_blocks, halo_blocks)], sem.at[1]),
        pltpu.make_async_copy(adj_hbm, adj, sem.at[2]),
        pltpu.make_async_copy(grad_hbm, grad, sem.at[3]),
    ]
    for load in loads:
        load.start()

    def clear(i, carry):
        acc[i] = jnp.zeros((side, width), jnp.float32)
        return carry

    lax.fori_loop(0, row_blocks + 1, clear, 0)
    wsum[...] = jnp.zeros_like(wsum)
    bsum[...] = jnp.zeros_like(bsum)
    for load in loads[:3]:
        load.wait()

    def kept(block, blocks=1):
        at = lax.broadcasted_iota(jnp.int32, (blocks * side, width), 0)
        return at < keep_to - block * side

    def mask(i, carry):
        ext[i] = jnp.where(kept(i), ext[i].astype(jnp.float32), 0.0).astype(ext.dtype)
        return carry

    lax.fori_loop(keep_to // side, row_blocks, mask, 0)

    unroll = 4
    trips = (count + unroll - 1) // unroll

    def forward(t, carry):
        for u in range(unroll):
            b = t * unroll + u
            to = jnp.where(b < count, rows[b], row_blocks)
            acc[to] += jnp.dot(adj[b], ext[cols[b]], preferred_element_type=jnp.float32)
        return carry

    lax.fori_loop(0, trips, forward, 0)
    loads[3].wait()

    def put(i):
        return pltpu.make_async_copy(
            out.at[pl.ds(i * step, step)], out_hbm.at[pl.ds(i * step, step)], out_sem.at[i]
        )

    tall = step * side

    def dense(i, carry):
        at = pl.ds(i * step, step)
        agg = acc[at].reshape(tall, width).astype(jnp.bfloat16)
        pre = jnp.dot(agg, w_ref[...], preferred_element_type=jnp.float32) + b_ref[...]
        keep = kept(i * step, step)
        sig = 0.5 * jnp.tanh(0.5 * pre) + 0.5
        act = pre * sig
        out[at] = jnp.where(keep, act, 0.0).astype(jnp.bfloat16).reshape(step, side, width)
        put(i).start()
        g = grad[at].reshape(tall, width).astype(jnp.float32)
        dpre = jnp.where(keep, g * (sig + act * (1.0 - sig)), 0.0).astype(jnp.bfloat16)
        wsum[...] += lax.dot_general(
            agg, dpre, (((0,), (0,)), ((), ())), preferred_element_type=jnp.float32
        )
        bsum[...] += jnp.sum(dpre.astype(jnp.float32).reshape(tall // 8, 8, width), 0)
        back[at] = (
            lax.dot_general(
                dpre, w_ref[...], (((1,), (1,)), ((), ())), preferred_element_type=jnp.float32
            )
            .astype(jnp.bfloat16)
            .reshape(step, side, width)
        )
        return carry

    lax.fori_loop(0, row_blocks // step, dense, 0)
    wg_ref[...] = wsum[...].astype(wg_ref.dtype)
    bg_ref[...] = jnp.sum(bsum[...], 0, keepdims=True)

    kept_back = pltpu.make_async_copy(back, back_hbm, sem.at[0])
    kept_back.start()
    kept_back.wait()

    def drain(i, carry):
        put(i).wait()
        return carry

    lax.fori_loop(0, row_blocks // step, drain, 0)


def back_kernel(
    n_wide,
    n_narrow,
    scale,
    table,
    nodes_live,
    idx_ref,
    wg_ref,
    bg_ref,
    adj_hbm,
    back_hbm,
    grad_ref,
    wout_ref,
    bout_ref,
    adj,
    back,
    run,
    ret,
    incoming,
    rs_wide,
    rs_narrow,
    part,
    ag_narrow,
    ag_wide,
    b_wide,
    b_mid,
    b_narrow,
    load,
    send,
    recv,
    send_w,
    recv_w,
    send_n,
    recv_n,
    send_gn,
    recv_gn,
    send_gw,
    recv_gw,
    send_bw,
    recv_bw,
    send_bn,
    recv_bn,
):
    w = lax.axis_index("wide")
    n = lax.axis_index("narrow")
    slab = wg_ref.shape[1]
    part_width = rs_narrow.shape[2]
    row_blocks, side, width = back.shape
    slots = adj.shape[0]
    loads = [
        pltpu.make_async_copy(back_hbm, back, load.at[0]),
        pltpu.make_async_copy(adj_hbm, adj, load.at[1]),
    ]
    for fetch in loads:
        fetch.start()

    def wide_peer(d):
        return (lax.rem(w + d, n_wide), n)

    def narrow_peer(d):
        return (w, lax.rem(n + d, n_narrow))

    peers = [wide_peer(d) for d in range(1, n_wide)] + [
        narrow_peer(d) for d in range(1, n_narrow)
    ]
    barrier = pltpu.get_barrier_semaphore()
    for peer in peers:
        pl.semaphore_signal(barrier, inc=1, device_id=peer, device_id_type=MESH)
    pl.semaphore_wait(barrier, len(peers))

    def remote(src, dst, s, r, peer):
        return pltpu.make_async_remote_copy(
            src_ref=src, dst_ref=dst, send_sem=s, recv_sem=r, device_id=peer, device_id_type=MESH
        )

    pending = []
    near = neighbours(n_wide, n_narrow)

    first = []
    for d in range(1, n_wide):
        peer = wide_peer(d)
        c = remote(wg_ref.at[peer[0]], rs_wide.at[d], send_w.at[d], recv_w.at[d], peer)
        c.start()
        first.append(c)
    bias_first = []
    for d in range(1, n_wide):
        c = remote(bg_ref, b_wide.at[d], send_bw.at[d], recv_bw.at[d], wide_peer(d))
        c.start()
        bias_first.append(c)
    run[0] = jnp.zeros(run.shape[1:], run.dtype)
    for fetch in loads:
        fetch.wait()
    unroll = 4

    def backward(t, carry):
        held = run[t * unroll]
        for u in range(unroll):
            k = t * unroll + u
            held = held * table[2, k].astype(jnp.float32) + lax.dot_general(
                adj[table[0, k]],
                back[table[1, k]],
                (((0,), (0,)), ((), ())),
                preferred_element_type=jnp.float32,
            )
            run[k + 1] = held
        return carry

    early = (slots - row_blocks) // unroll
    lax.fori_loop(0, early, backward, 0)
    halo_blocks = ret.shape[0] * ret.shape[1] // side
    per = ret.shape[1] // side
    for k in (2, 3, 1, 0):
        there, target = near[k]
        for j in range(per):
            ret[k, pl.ds(j * side, side), :] = run[table[3, k * per + j]].astype(ret.dtype)

        @pl.when(there)
        def _():
            halo_copy(ret, incoming, send, recv, k, target).start()

        @pl.when(jnp.logical_not(there))
        def _():
            incoming[k] = jnp.zeros(incoming.shape[1:], incoming.dtype)

    total = wg_ref[w].astype(jnp.float32)
    for c in first:
        c.wait_recv()
    for d in range(1, n_wide):
        total = total + rs_wide[d].astype(jnp.float32)
    bias = bg_ref[...]
    for c in bias_first:
        c.wait_recv()
    for d in range(1, n_wide):
        bias = bias + b_wide[d]
    b_mid[...] = bias
    for j in range(n_narrow):
        part[j] = total[:, j * part_width : (j + 1) * part_width].astype(part.dtype)
    second = []
    for d in range(1, n_narrow):
        peer = narrow_peer(d)
        c = remote(part.at[peer[1]], rs_narrow.at[d], send_n.at[d], recv_n.at[d], peer)
        c.start()
        second.append(c)
    for d in range(1, n_narrow):
        c = remote(b_mid, b_narrow.at[d], send_bn.at[d], recv_bn.at[d], narrow_peer(d))
        c.start()
        bias_first.append(c)
        second.append(c)
    lax.fori_loop(early, slots // unroll, backward, 0)
    piece = part[n].astype(jnp.float32)
    for c in second:
        c.wait_recv()
    for d in range(1, n_narrow):
        piece = piece + rs_narrow[d].astype(jnp.float32)
        bias = bias + b_narrow[d]
    bout_ref[...] = bias * scale
    ag_narrow[n] = (piece * scale).astype(ag_narrow.dtype)
    third = []
    for d in range(1, n_narrow):
        c = remote(
            ag_narrow.at[n], ag_narrow.at[n], send_gn.at[d], recv_gn.at[d], narrow_peer(d)
        )
        c.start()
        third.append(c)
    chunk = grad_ref.shape[1]
    across = chunk // side
    keep_to = nodes_live[0]

    def own(i):
        return jnp.concatenate(
            [run[table[3, halo_blocks + i * across + j]] for j in range(across)], 0
        )

    def finish(i, full):
        row = lax.broadcasted_iota(jnp.int32, full.shape, 0) + i * chunk
        grad_ref[i] = jnp.where(row < keep_to, full, 0.0).astype(grad_ref.dtype)

    low_chunks = row_blocks // across // 2

    def high(i, carry):
        finish(i, own(i))
        return carry

    lax.fori_loop(low_chunks, row_blocks // across, high, 0)
    for c in third:
        c.wait_recv()
    fourth = []
    for d in range(1, n_wide):
        c = remote(ag_narrow, ag_wide.at[w], send_gw.at[d], recv_gw.at[d], wide_peer(d))
        c.start()
        fourth.append(c)
    ag_wide[w] = ag_narrow[...]

    for k in range(4):
        there, target = near[k]

        @pl.when(there)
        def _():
            halo_copy(ret, incoming, send, recv, k, target).wait_send()
            halo_copy(ret, incoming, send, recv, k ^ 1, target).wait_recv()

    merged = incoming[...].reshape(-1, width)
    idx = idx_ref[...]

    def scatter(i, carry):
        at = lax.broadcasted_iota(jnp.int32, (chunk, idx.shape[1]), 0) + i * chunk
        hot = jnp.where(at == idx, 1.0, 0.0).astype(jnp.bfloat16)
        finish(i, own(i) + jnp.dot(hot, merged, preferred_element_type=jnp.float32))
        return carry

    lax.fori_loop(0, low_chunks, scatter, 0)
    for c in fourth:
        c.wait_recv()
    for i in range(n_wide):
        for j in range(n_narrow):
            wout_ref[pl.ds(i * slab, slab), pl.ds(j * part_width, part_width)] = ag_wide[
                i, j
            ].astype(jnp.float32)
    for c in first + bias_first + second[: n_narrow - 1] + third + fourth:
        c.wait_send()


def local(
    n_wide,
    n_narrow,
    features,
    adjacency,
    block_rows,
    block_cols,
    block_count,
    node_count,
    halo_index,
    weight,
    bias,
    out_grad,
):
    nodes, width = features.shape
    slots, side, _ = adjacency.shape
    row_blocks = nodes // side
    sides, halo = halo_index.shape[1:]
    halo_blocks = sides * halo // side
    col_blocks = row_blocks + halo_blocks
    bf, f32 = jnp.bfloat16, jnp.float32
    picks = halo_index[0]
    vm = pl.BlockSpec(memory_space=pltpu.VMEM)
    sm = pl.BlockSpec(memory_space=pltpu.SMEM)
    hb = pl.BlockSpec(memory_space=ANY)
    dma = pltpu.SemaphoreType.DMA

    lanes = -(-slots // 128) * 128
    pad = ((0, 0), (0, lanes - slots))
    halos, table = pl.pallas_call(
        functools.partial(gather_kernel, n_wide, n_narrow, row_blocks, col_blocks),
        name="halo_out",
        out_shape=(
            jax.ShapeDtypeStruct((sides, halo, width), bf),
            jax.ShapeDtypeStruct((8, lanes), jnp.int32),
        ),
        in_specs=[vm, vm, vm, vm, hb],
        out_specs=(vm, vm),
        scratch_shapes=[
            pltpu.VMEM((nodes // 2, width), bf),
            pltpu.VMEM((sides, halo, width), bf),
            dma,
            dma((sides,)),
            dma((sides,)),
        ],
        compiler_params=pltpu.CompilerParams(
            collective_id=0, has_side_effects=True, vmem_limit_bytes=VMEM_LIMIT
        ),
    )(
        picks,
        jnp.pad(block_rows, pad),
        jnp.pad(block_cols, pad),
        jnp.broadcast_to(block_count[:, None], (1, lanes)),
        features,
    )

    step = 2
    blocked = (row_blocks, side, width)
    out, back, wg, bg = pl.pallas_call(
        functools.partial(layer_kernel, step),
        name="layer",
        out_shape=(
            jax.ShapeDtypeStruct(blocked, bf),
            jax.ShapeDtypeStruct(blocked, bf),
            jax.ShapeDtypeStruct((width, width), bf),
            jax.ShapeDtypeStruct((1, width), f32),
        ),
        in_specs=[sm, sm, sm, sm, hb, hb, hb, hb, vm, vm],
        out_specs=(hb, hb, vm, vm),
        scratch_shapes=[
            pltpu.VMEM((col_blocks, side, width), bf),
            pltpu.VMEM((slots, side, side), bf),
            pltpu.VMEM(blocked, bf),
            pltpu.VMEM((row_blocks + 1, side, width), f32),
            pltpu.VMEM(blocked, bf),
            pltpu.VMEM(blocked, bf),
            pltpu.VMEM((width, width), f32),
            pltpu.VMEM((8, width), f32),
            dma((4,)),
            dma((row_blocks // step,)),
        ],
        compiler_params=pltpu.CompilerParams(vmem_limit_bytes=VMEM_LIMIT),
    )(
        block_rows[0],
        block_cols[0],
        block_count,
        node_count,
        features.reshape(blocked),
        halos.reshape(halo_blocks, side, width),
        adjacency,
        out_grad.reshape(blocked),
        weight,
        bias.reshape(1, width),
    )

    slab = width // n_wide
    part_width = width // n_narrow
    scale = 1.0 / math.sqrt(nodes * n_wide * n_narrow)
    chunk = 2 * side
    input_grad, wout, bout = pl.pallas_call(
        functools.partial(back_kernel, n_wide, n_narrow, scale),
        name="back",
        out_shape=(
            jax.ShapeDtypeStruct((nodes // chunk, chunk, width), bf),
            jax.ShapeDtypeStruct((width, width), f32),
            jax.ShapeDtypeStruct((1, width), f32),
        ),
        in_specs=[sm, sm, vm, vm, vm, hb, hb],
        out_specs=(vm, vm, vm),
        scratch_shapes=[
            pltpu.VMEM((slots, side, side), bf),
            pltpu.VMEM(blocked, bf),
            pltpu.VMEM((slots + 1, side, width), f32),
            pltpu.VMEM((sides, halo, width), bf),
            pltpu.VMEM((sides, halo, width), bf),
            pltpu.VMEM((n_wide, slab, width), bf),
            pltpu.VMEM((n_narrow, slab, part_width), bf),
            pltpu.VMEM((n_narrow, slab, part_width), bf),
            pltpu.VMEM((n_narrow, slab, part_width), bf),
            pltpu.VMEM((n_wide, n_narrow, slab, part_width), bf),
            pltpu.VMEM((n_wide, 1, width), f32),
            pltpu.VMEM((1, width), f32),
            pltpu.VMEM((n_narrow, 1, width), f32),
            dma((2,)),
            dma((sides,)),
            dma((sides,)),
        ]
        + [dma((n_wide,))] * 2
        + [dma((n_narrow,))] * 4
        + [dma((n_wide,))] * 4
        + [dma((n_narrow,))] * 2,
        compiler_params=pltpu.CompilerParams(
            collective_id=1, has_side_effects=True, vmem_limit_bytes=VMEM_LIMIT
        ),
    )(
        table,
        node_count,
        picks.reshape(1, sides * halo),
        wg.reshape(n_wide, slab, width),
        bg,
        adjacency,
        back,
    )
    return out.reshape(nodes, width), input_grad.reshape(nodes, width), wout, bout.reshape(width)


def solution(mesh):
    both = ("wide", "narrow")
    placed = (
        P(both, None),
        P(both, None, None),
        P(both, None),
        P(both, None),
        P(both),
        P(both),
        P(both, None, None),
        P(),
        P(),
        P(both, None),
    )
    return jax.shard_map(
        functools.partial(local, mesh.shape["wide"], mesh.shape["narrow"]),
        mesh=mesh,
        in_specs=placed,
        out_specs=(P(both, None), P(both, None), P(), P()),
        check_vma=False,
    )
```

```python
import functools
import math

import jax
import jax.numpy as jnp
from jax import lax
from jax.experimental import pallas as pl
from jax.experimental.pallas import tpu as pltpu
from jax.sharding import PartitionSpec as P

MESH = pl.DeviceIdType.MESH
ANY = pl.ANY
VMEM_LIMIT = 60 * 1024 * 1024


def neighbours(n_wide, n_narrow):
    w = lax.axis_index("wide")
    n = lax.axis_index("narrow")
    return (
        (w > 0, (w - 1, n)),
        (w < n_wide - 1, (w + 1, n)),
        (n > 0, (w, n - 1)),
        (n < n_narrow - 1, (w, n + 1)),
    )


def halo_copy(src, dst, send, recv, k, target):
    return pltpu.make_async_remote_copy(
        src_ref=src.at[k],
        dst_ref=dst.at[k ^ 1],
        send_sem=send.at[k],
        recv_sem=recv.at[k ^ 1],
        device_id=target,
        device_id_type=MESH,
    )


def tables(row_ref, col_ref, pads, count, row_blocks, col_blocks):
    lanes = pads.shape[1]
    slots = row_ref.shape[1]
    f32 = jnp.float32
    pads[...] = jnp.zeros_like(pads)
    pads[0:1, 0:slots] = row_ref[...]
    pads[1:2, 0:slots] = col_ref[...]
    lane = lax.broadcasted_iota(jnp.int32, (lanes, lanes), 1).astype(f32)
    sub = lax.broadcasted_iota(jnp.int32, (lanes, lanes), 0).astype(f32)

    def spread(x):
        return jnp.broadcast_to(x.astype(f32), (lanes, lanes))

    halo_blocks = col_blocks - row_blocks
    col = spread(pads[1:2, :])
    place = jnp.where(col >= row_blocks, col - row_blocks, col + halo_blocks)
    place = jnp.where(lane < count.astype(f32), place, float(col_blocks))
    place_t = jnp.transpose(place)
    row_t = jnp.transpose(spread(pads[0:1, :]))
    same = place == place_t
    ahead = lane < sub
    one = lambda m: jnp.where(m, 1.0, 0.0)
    rank = jnp.sum(one((place < place_t) | (same & ahead)), 1, keepdims=True)
    twin = jnp.minimum(jnp.sum(one(same & ahead), 1, keepdims=True), 1.0)
    hot = one(jnp.broadcast_to(rank, (lanes, lanes)) == lane)
    pick = lambda x: jnp.sum(hot * x, 0, keepdims=True)
    ends = jnp.sum(one(place_t <= lane), 0, keepdims=True)
    keep = pick(jnp.broadcast_to(twin, (lanes, lanes)))
    return pick(sub), pick(row_t), keep, ends


def gather_kernel(
    n_wide,
    n_narrow,
    row_blocks,
    col_blocks,
    idx_ref,
    row_ref,
    col_ref,
    count_ref,
    feat_hbm,
    halo_ref,
    table_ref,
    pads,
    feat,
    packed,
    load,
    send,
    recv,
):
    count = idx_ref.shape[2]
    span = feat.shape[0]
    fetch = pltpu.make_async_copy(feat_hbm.at[pl.ds(0, span)], feat, load)
    fetch.start()
    near = neighbours(n_wide, n_narrow)
    barrier = pltpu.get_barrier_semaphore()
    for there, target in near:

        @pl.when(there)
        def _():
            pl.semaphore_signal(barrier, inc=1, device_id=target, device_id_type=MESH)

    fetch.wait()
    lane = lax.broadcasted_iota(jnp.int32, (count, 128), 1).astype(jnp.float32)

    def pack(k):
        row = idx_ref[0, pl.ds(k, 1), :].astype(jnp.float32)
        column = jnp.transpose(jnp.broadcast_to(row, (128, count)))
        hot = jnp.concatenate(
            [
                jnp.where(column == lane + float(at), 1.0, 0.0).astype(jnp.bfloat16)
                for at in range(0, span, 128)
            ],
            axis=1,
        )
        packed[k] = jnp.dot(hot, feat[...], preferred_element_type=jnp.float32).astype(
            jnp.bfloat16
        )

    pack(2)
    pl.semaphore_wait(barrier, sum(there.astype(jnp.int32) for there, _ in near))
    for k in (2, 3, 1, 0):
        there, target = near[k]
        if k != 2:
            pack(k)

        @pl.when(there)
        def _():
            halo_copy(packed, halo_ref, send, recv, k, target).start()

        @pl.when(jnp.logical_not(there))
        def _():
            halo_ref[k] = jnp.zeros(halo_ref.shape[1:], halo_ref.dtype)

    table_ref[...] = jnp.zeros_like(table_ref)
    for i, line in enumerate(
        tables(row_ref, col_ref, pads, count_ref[0], row_blocks, col_blocks)
    ):
        table_ref[pl.ds(i, 1), :] = line.astype(jnp.int32)

    for k in range(4):
        there, target = near[k]

        @pl.when(there)
        def _():
            halo_copy(packed, halo_ref, send, recv, k, target).wait_send()
            halo_copy(packed, halo_ref, send, recv, k ^ 1, target).wait_recv()


def layer_kernel(
    step,
    rows,
    cols,
    live,
    nodes_live,
    feat_hbm,
    halo_hbm,
    adj_hbm,
    grad_hbm,
    w_ref,
    b_ref,
    out_hbm,
    back_hbm,
    wg_ref,
    bg_ref,
    ext,
    adj,
    grad,
    acc,
    back,
    out,
    wsum,
    bsum,
    sem,
    out_sem,
):
    row_blocks, side, width = feat_hbm.shape
    halo_blocks = halo_hbm.shape[0]
    count = live[0]
    keep_to = nodes_live[0]
    loads = [
        pltpu.make_async_copy(feat_hbm, ext.at[pl.ds(0, row_blocks)], sem.at[0]),
        pltpu.make_async_copy(halo_hbm, ext.at[pl.ds(row_blocks, halo_blocks)], sem.at[1]),
        pltpu.make_async_copy(adj_hbm, adj, sem.at[2]),
        pltpu.make_async_copy(grad_hbm, grad, sem.at[3]),
    ]
    for load in loads:
        load.start()

    def clear(i, carry):
        acc[i] = jnp.zeros((side, width), jnp.float32)
        return carry

    lax.fori_loop(0, row_blocks + 1, clear, 0)
    wsum[...] = jnp.zeros_like(wsum)
    bsum[...] = jnp.zeros_like(bsum)
    for load in loads[:3]:
        load.wait()

    def kept(block, blocks=1):
        at = lax.broadcasted_iota(jnp.int32, (blocks * side, width), 0)
        return at < keep_to - block * side

    def mask(i, carry):
        ext[i] = jnp.where(kept(i), ext[i].astype(jnp.float32), 0.0).astype(ext.dtype)
        return carry

    lax.fori_loop(keep_to // side, row_blocks, mask, 0)

    unroll = 4
    trips = (count + unroll - 1) // unroll

    def forward(t, carry):
        for u in range(unroll):
            b = t * unroll + u
            to = jnp.where(b < count, rows[b], row_blocks)
            acc[to] += jnp.dot(adj[b], ext[cols[b]], preferred_element_type=jnp.float32)
        return carry

    lax.fori_loop(0, trips, forward, 0)
    loads[3].wait()

    def put(i):
        return pltpu.make_async_copy(
            out.at[pl.ds(i * step, step)], out_hbm.at[pl.ds(i * step, step)], out_sem.at[i]
        )

    tall = step * side

    def into(i):
        at = pl.ds(i * step, step)
        agg = acc[at].reshape(tall, width).astype(jnp.bfloat16)
        return agg, jnp.dot(agg, w_ref[...], preferred_element_type=jnp.float32)

    def middle(i, pre):
        at = pl.ds(i * step, step)
        pre = pre + b_ref[...]
        keep = kept(i * step, step)
        sig = 0.5 * jnp.tanh(0.5 * pre) + 0.5
        act = pre * sig
        out[at] = jnp.where(keep, act, 0.0).astype(jnp.bfloat16).reshape(step, side, width)
        put(i).start()
        g = grad[at].reshape(tall, width).astype(jnp.float32)
        dpre = jnp.where(keep, g * (sig + act * (1.0 - sig)), 0.0).astype(jnp.bfloat16)
        bsum[...] += jnp.sum(dpre.astype(jnp.float32).reshape(tall // 8, 8, width), 0)
        return dpre

    def after(i, agg, dpre):
        wsum[...] += lax.dot_general(
            agg, dpre, (((0,), (0,)), ((), ())), preferred_element_type=jnp.float32
        )
        back[pl.ds(i * step, step)] = (
            lax.dot_general(
                dpre, w_ref[...], (((1,), (1,)), ((), ())), preferred_element_type=jnp.float32
            )
            .astype(jnp.bfloat16)
            .reshape(step, side, width)
        )

    group = 4

    def dense(t, carry):
        now = into(t * group)
        for u in range(group):
            i = t * group + u
            later = into(i + 1) if u + 1 < group else None
            dpre = middle(i, now[1])
            after(i, now[0], dpre)
            now = later
        return carry

    lax.fori_loop(0, row_blocks // step // group, dense, 0)
    wg_ref[...] = wsum[...].astype(wg_ref.dtype)
    bg_ref[...] = jnp.sum(bsum[...], 0, keepdims=True)

    kept_back = pltpu.make_async_copy(back, back_hbm, sem.at[0])
    kept_back.start()
    kept_back.wait()

    def drain(i, carry):
        put(i).wait()
        return carry

    lax.fori_loop(0, row_blocks // step, drain, 0)


def back_kernel(
    n_wide,
    n_narrow,
    scale,
    table,
    nodes_live,
    idx_ref,
    wg_ref,
    bg_ref,
    adj_hbm,
    back_hbm,
    grad_hbm,
    wout_ref,
    bout_ref,
    grad_ref,
    grad_sem,
    adj,
    back,
    run,
    ret,
    incoming,
    rs_wide,
    rs_narrow,
    part,
    ag_narrow,
    ag_wide,
    b_wide,
    b_mid,
    b_narrow,
    load,
    send,
    recv,
    send_w,
    recv_w,
    send_n,
    recv_n,
    send_gn,
    recv_gn,
    send_gw,
    recv_gw,
    send_bw,
    recv_bw,
    send_bn,
    recv_bn,
):
    w = lax.axis_index("wide")
    n = lax.axis_index("narrow")
    slab = wg_ref.shape[1]
    part_width = rs_narrow.shape[2]
    row_blocks, side, width = back.shape
    slots = adj.shape[0]
    loads = [
        pltpu.make_async_copy(back_hbm, back, load.at[0]),
        pltpu.make_async_copy(adj_hbm, adj, load.at[1]),
    ]
    for fetch in loads:
        fetch.start()

    def wide_peer(d):
        return (lax.rem(w + d, n_wide), n)

    def narrow_peer(d):
        return (w, lax.rem(n + d, n_narrow))

    peers = [wide_peer(d) for d in range(1, n_wide)] + [
        narrow_peer(d) for d in range(1, n_narrow)
    ]
    barrier = pltpu.get_barrier_semaphore()
    for peer in peers:
        pl.semaphore_signal(barrier, inc=1, device_id=peer, device_id_type=MESH)
    pl.semaphore_wait(barrier, len(peers))

    def remote(src, dst, s, r, peer):
        return pltpu.make_async_remote_copy(
            src_ref=src, dst_ref=dst, send_sem=s, recv_sem=r, device_id=peer, device_id_type=MESH
        )

    pending = []
    near = neighbours(n_wide, n_narrow)

    first = []
    for d in range(1, n_wide):
        peer = wide_peer(d)
        c = remote(wg_ref.at[peer[0]], rs_wide.at[d], send_w.at[d], recv_w.at[d], peer)
        c.start()
        first.append(c)
    bias_first = []
    for d in range(1, n_wide):
        c = remote(bg_ref, b_wide.at[d], send_bw.at[d], recv_bw.at[d], wide_peer(d))
        c.start()
        bias_first.append(c)
    run[0] = jnp.zeros(run.shape[1:], run.dtype)
    for fetch in loads:
        fetch.wait()
    unroll = 4

    def backward(t, carry):
        held = run[t * unroll]
        for u in range(unroll):
            k = t * unroll + u
            held = held * table[2, k].astype(jnp.float32) + lax.dot_general(
                adj[table[0, k]],
                back[table[1, k]],
                (((0,), (0,)), ((), ())),
                preferred_element_type=jnp.float32,
            )
            run[k + 1] = held
        return carry

    early = (slots - row_blocks) // unroll
    lax.fori_loop(0, early, backward, 0)
    halo_blocks = ret.shape[0] * ret.shape[1] // side
    per = ret.shape[1] // side
    for k in (2, 3, 1, 0):
        there, target = near[k]
        for j in range(per):
            ret[k, pl.ds(j * side, side), :] = run[table[3, k * per + j]].astype(ret.dtype)

        @pl.when(there)
        def _():
            halo_copy(ret, incoming, send, recv, k, target).start()

        @pl.when(jnp.logical_not(there))
        def _():
            incoming[k] = jnp.zeros(incoming.shape[1:], incoming.dtype)

    total = wg_ref[w].astype(jnp.float32)
    for c in first:
        c.wait_recv()
    for d in range(1, n_wide):
        total = total + rs_wide[d].astype(jnp.float32)
    bias = bg_ref[...]
    for c in bias_first:
        c.wait_recv()
    for d in range(1, n_wide):
        bias = bias + b_wide[d]
    b_mid[...] = bias
    for j in range(n_narrow):
        part[j] = total[:, j * part_width : (j + 1) * part_width].astype(part.dtype)
    second = []
    for d in range(1, n_narrow):
        peer = narrow_peer(d)
        c = remote(part.at[peer[1]], rs_narrow.at[d], send_n.at[d], recv_n.at[d], peer)
        c.start()
        second.append(c)
    for d in range(1, n_narrow):
        c = remote(b_mid, b_narrow.at[d], send_bn.at[d], recv_bn.at[d], narrow_peer(d))
        c.start()
        bias_first.append(c)
        second.append(c)
    lax.fori_loop(early, slots // unroll, backward, 0)
    piece = part[n].astype(jnp.float32)
    for c in second:
        c.wait_recv()
    for d in range(1, n_narrow):
        piece = piece + rs_narrow[d].astype(jnp.float32)
        bias = bias + b_narrow[d]
    bout_ref[...] = bias * scale
    ag_narrow[n] = (piece * scale).astype(ag_narrow.dtype)
    third = []
    for d in range(1, n_narrow):
        c = remote(
            ag_narrow.at[n], ag_narrow.at[n], send_gn.at[d], recv_gn.at[d], narrow_peer(d)
        )
        c.start()
        third.append(c)
    chunk = grad_ref.shape[1]
    across = chunk // side
    keep_to = nodes_live[0]

    def own(i):
        return jnp.concatenate(
            [run[table[3, halo_blocks + i * across + j]] for j in range(across)], 0
        )

    def leave(i):
        return pltpu.make_async_copy(grad_ref.at[i], grad_hbm.at[i], grad_sem.at[i])

    def finish(i, full):
        row = lax.broadcasted_iota(jnp.int32, full.shape, 0) + i * chunk
        grad_ref[i] = jnp.where(row < keep_to, full, 0.0).astype(grad_ref.dtype)
        leave(i).start()

    low_chunks = row_blocks // across // 2

    def high(i, carry):
        finish(i, own(i))
        return carry

    lax.fori_loop(low_chunks, row_blocks // across, high, 0)
    for c in third:
        c.wait_recv()
    fourth = []
    for d in range(1, n_wide):
        c = remote(ag_narrow, ag_wide.at[w], send_gw.at[d], recv_gw.at[d], wide_peer(d))
        c.start()
        fourth.append(c)
    ag_wide[w] = ag_narrow[...]

    for k in range(4):
        there, target = near[k]

        @pl.when(there)
        def _():
            halo_copy(ret, incoming, send, recv, k, target).wait_send()
            halo_copy(ret, incoming, send, recv, k ^ 1, target).wait_recv()

    merged = incoming[...].reshape(-1, width)
    idx = jnp.concatenate([idx_ref[0, k : k + 1, :] for k in range(4)], 1)

    def scatter(i, carry):
        at = lax.broadcasted_iota(jnp.int32, (chunk, idx.shape[1]), 0) + i * chunk
        hot = jnp.where(at == idx, 1.0, 0.0).astype(jnp.bfloat16)
        finish(i, own(i) + jnp.dot(hot, merged, preferred_element_type=jnp.float32))
        return carry

    lax.fori_loop(0, low_chunks, scatter, 0)
    for c in fourth:
        c.wait_recv()
    for i in range(n_wide):
        for j in range(n_narrow):
            wout_ref[pl.ds(i * slab, slab), pl.ds(j * part_width, part_width)] = ag_wide[
                i, j
            ].astype(jnp.float32)
    def drain(i, carry):
        leave(i).wait()
        return carry

    lax.fori_loop(0, row_blocks // across, drain, 0)
    for c in first + bias_first + second[: n_narrow - 1] + third + fourth:
        c.wait_send()


def hand_on(grad_in, w_in, b_in, grad_out, w_out, b_out, grad, wg, bg, take, give):
    pieces = grad.shape[0]
    hops = [(grad_in.at[i], grad.at[i], grad_out.at[i]) for i in range(pieces)]
    hops += [(w_in, wg, w_out), (b_in, bg, b_out)]
    ins = [pltpu.make_async_copy(a, b, take.at[i]) for i, (a, b, _) in enumerate(hops)]
    outs = [pltpu.make_async_copy(b, c, give.at[i]) for i, (_, b, c) in enumerate(hops)]
    for c in ins:
        c.start()
    for c, d in zip(ins, outs):
        c.wait()
        d.start()
    for d in outs:
        d.wait()


def local(
    n_wide,
    n_narrow,
    features,
    adjacency,
    block_rows,
    block_cols,
    block_count,
    node_count,
    halo_index,
    weight,
    bias,
    out_grad,
):
    nodes, width = features.shape
    slots, side, _ = adjacency.shape
    row_blocks = nodes // side
    sides, halo = halo_index.shape[1:]
    halo_blocks = sides * halo // side
    col_blocks = row_blocks + halo_blocks
    bf, f32 = jnp.bfloat16, jnp.float32
    vm = pl.BlockSpec(memory_space=pltpu.VMEM)
    sm = pl.BlockSpec(memory_space=pltpu.SMEM)
    hb = pl.BlockSpec(memory_space=ANY)
    dma = pltpu.SemaphoreType.DMA

    lanes = -(-slots // 128) * 128
    halos, table = pl.pallas_call(
        functools.partial(gather_kernel, n_wide, n_narrow, row_blocks, col_blocks),
        name="halo_out",
        out_shape=(
            jax.ShapeDtypeStruct((sides, halo, width), bf),
            jax.ShapeDtypeStruct((8, lanes), jnp.int32),
        ),
        in_specs=[vm, vm, vm, sm, hb],
        out_specs=(vm, vm),
        scratch_shapes=[
            pltpu.VMEM((8, lanes), jnp.int32),
            pltpu.VMEM((nodes // 2, width), bf),
            pltpu.VMEM((sides, halo, width), bf),
            dma,
            dma((sides,)),
            dma((sides,)),
        ],
        compiler_params=pltpu.CompilerParams(
            collective_id=0, has_side_effects=True, vmem_limit_bytes=VMEM_LIMIT
        ),
    )(
        halo_index,
        block_rows,
        block_cols,
        block_count,
        features,
    )

    step = 2
    blocked = (row_blocks, side, width)
    out, back, wg, bg = pl.pallas_call(
        functools.partial(layer_kernel, step),
        name="layer",
        out_shape=(
            jax.ShapeDtypeStruct(blocked, bf),
            jax.ShapeDtypeStruct(blocked, bf),
            jax.ShapeDtypeStruct((width, width), bf),
            jax.ShapeDtypeStruct((1, width), f32),
        ),
        in_specs=[sm, sm, sm, sm, hb, hb, hb, hb, vm, vm],
        out_specs=(hb, hb, vm, vm),
        scratch_shapes=[
            pltpu.VMEM((col_blocks, side, width), bf),
            pltpu.VMEM((slots, side, side), bf),
            pltpu.VMEM(blocked, bf),
            pltpu.VMEM((row_blocks + 1, side, width), f32),
            pltpu.VMEM(blocked, bf),
            pltpu.VMEM(blocked, bf),
            pltpu.VMEM((width, width), f32),
            pltpu.VMEM((8, width), f32),
            dma((4,)),
            dma((row_blocks // step,)),
        ],
        compiler_params=pltpu.CompilerParams(vmem_limit_bytes=VMEM_LIMIT),
    )(
        block_rows[0],
        block_cols[0],
        block_count,
        node_count,
        features.reshape(blocked),
        halos.reshape(halo_blocks, side, width),
        adjacency,
        out_grad.reshape(blocked),
        weight,
        bias.reshape(1, width),
    )

    slab = width // n_wide
    part_width = width // n_narrow
    scale = 1.0 / math.sqrt(nodes * n_wide * n_narrow)
    chunk = 2 * side
    input_grad, wout, bout = pl.pallas_call(
        functools.partial(back_kernel, n_wide, n_narrow, scale),
        name="back",
        out_shape=(
            jax.ShapeDtypeStruct((nodes // chunk, chunk, width), bf),
            jax.ShapeDtypeStruct((width, width), f32),
            jax.ShapeDtypeStruct((1, width), f32),
        ),
        in_specs=[sm, sm, vm, vm, vm, hb, hb],
        out_specs=(hb, vm, vm),
        scratch_shapes=[
            pltpu.VMEM((nodes // chunk, chunk, width), bf),
            dma((nodes // chunk,)),
            pltpu.VMEM((slots, side, side), bf),
            pltpu.VMEM(blocked, bf),
            pltpu.VMEM((slots + 1, side, width), f32),
            pltpu.VMEM((sides, halo, width), bf),
            pltpu.VMEM((sides, halo, width), bf),
            pltpu.VMEM((n_wide, slab, width), bf),
            pltpu.VMEM((n_narrow, slab, part_width), bf),
            pltpu.VMEM((n_narrow, slab, part_width), bf),
            pltpu.VMEM((n_narrow, slab, part_width), bf),
            pltpu.VMEM((n_wide, n_narrow, slab, part_width), bf),
            pltpu.VMEM((n_wide, 1, width), f32),
            pltpu.VMEM((1, width), f32),
            pltpu.VMEM((n_narrow, 1, width), f32),
            dma((2,)),
            dma((sides,)),
            dma((sides,)),
        ]
        + [dma((n_wide,))] * 2
        + [dma((n_narrow,))] * 4
        + [dma((n_wide,))] * 4
        + [dma((n_narrow,))] * 2,
        compiler_params=pltpu.CompilerParams(
            collective_id=1, has_side_effects=True, vmem_limit_bytes=VMEM_LIMIT
        ),
    )(
        table,
        node_count,
        halo_index,
        wg.reshape(n_wide, slab, width),
        bg,
        adjacency,
        back,
    )
    pieces = 8
    input_grad, wout, bout = pl.pallas_call(
        hand_on,
        name="hand_on",
        out_shape=(
            jax.ShapeDtypeStruct((pieces, nodes // pieces, width), bf),
            jax.ShapeDtypeStruct((width, width), f32),
            jax.ShapeDtypeStruct((1, width), f32),
        ),
        in_specs=[hb, hb, hb],
        out_specs=(hb, hb, hb),
        scratch_shapes=[
            pltpu.VMEM((pieces, nodes // pieces, width), bf),
            pltpu.VMEM((width, width), f32),
            pltpu.VMEM((1, width), f32),
            dma((pieces + 2,)),
            dma((pieces + 2,)),
        ],
        compiler_params=pltpu.CompilerParams(vmem_limit_bytes=VMEM_LIMIT),
    )(input_grad.reshape(pieces, nodes // pieces, width), wout, bout)
    return out.reshape(nodes, width), input_grad.reshape(nodes, width), wout, bout.reshape(width)


def solution(mesh):
    both = ("wide", "narrow")
    placed = (
        P(both, None),
        P(both, None, None),
        P(both, None),
        P(both, None),
        P(both),
        P(both),
        P(both, None, None),
        P(),
        P(),
        P(both, None),
    )
    return jax.shard_map(
        functools.partial(local, mesh.shape["wide"], mesh.shape["narrow"]),
        mesh=mesh,
        in_specs=placed,
        out_specs=(P(both, None), P(both, None), P(), P()),
        check_vma=False,
    )
```

```python
import functools
import math

import jax
import jax.numpy as jnp
from jax import lax
from jax.experimental import pallas as pl
from jax.experimental.pallas import tpu as pltpu
from jax.sharding import PartitionSpec as P

MESH = pl.DeviceIdType.MESH
ANY = pl.ANY
VMEM_LIMIT = 60 * 1024 * 1024


def neighbours(n_wide, n_narrow):
    w = lax.axis_index("wide")
    n = lax.axis_index("narrow")
    return (
        (w > 0, (w - 1, n)),
        (w < n_wide - 1, (w + 1, n)),
        (n > 0, (w, n - 1)),
        (n < n_narrow - 1, (w, n + 1)),
    )


def halo_copy(src, dst, send, recv, k, target):
    return pltpu.make_async_remote_copy(
        src_ref=src.at[k],
        dst_ref=dst.at[k ^ 1],
        send_sem=send.at[k],
        recv_sem=recv.at[k ^ 1],
        device_id=target,
        device_id_type=MESH,
    )


def tables(row_ref, col_ref, pads, count, row_blocks, col_blocks):
    lanes = pads.shape[1]
    slots = row_ref.shape[1]
    f32 = jnp.float32
    pads[...] = jnp.zeros_like(pads)
    pads[0:1, 0:slots] = row_ref[...]
    pads[1:2, 0:slots] = col_ref[...]
    lane = lax.broadcasted_iota(jnp.int32, (lanes, lanes), 1).astype(f32)
    sub = lax.broadcasted_iota(jnp.int32, (lanes, lanes), 0).astype(f32)

    def spread(x):
        return jnp.broadcast_to(x.astype(f32), (lanes, lanes))

    halo_blocks = col_blocks - row_blocks
    col = spread(pads[1:2, :])
    place = jnp.where(col >= row_blocks, col - row_blocks, col + halo_blocks)
    place = jnp.where(lane < count.astype(f32), place, float(col_blocks))
    place_t = jnp.transpose(place)
    row_t = jnp.transpose(spread(pads[0:1, :]))
    same = place == place_t
    ahead = lane < sub
    one = lambda m: jnp.where(m, 1.0, 0.0)
    rank = jnp.sum(one((place < place_t) | (same & ahead)), 1, keepdims=True)
    twin = jnp.minimum(jnp.sum(one(same & ahead), 1, keepdims=True), 1.0)
    hot = one(jnp.broadcast_to(rank, (lanes, lanes)) == lane)
    pick = lambda x: jnp.sum(hot * x, 0, keepdims=True)
    ends = jnp.sum(one(place_t <= lane), 0, keepdims=True)
    keep = pick(jnp.broadcast_to(twin, (lanes, lanes)))
    return pick(sub), pick(row_t), keep, ends


def gather_kernel(
    n_wide,
    n_narrow,
    row_blocks,
    col_blocks,
    idx_ref,
    row_ref,
    col_ref,
    count_ref,
    feat_hbm,
    halo_ref,
    table_ref,
    pads,
    feat,
    packed,
    load,
    send,
    recv,
):
    count = idx_ref.shape[2]
    span = feat.shape[0]
    fetch = pltpu.make_async_copy(feat_hbm.at[pl.ds(0, span)], feat, load)
    fetch.start()
    near = neighbours(n_wide, n_narrow)
    barrier = pltpu.get_barrier_semaphore()
    for there, target in near:

        @pl.when(there)
        def _():
            pl.semaphore_signal(barrier, inc=1, device_id=target, device_id_type=MESH)

    fetch.wait()
    lane = lax.broadcasted_iota(jnp.int32, (count, 128), 1).astype(jnp.float32)

    def pack(k):
        row = idx_ref[0, pl.ds(k, 1), :].astype(jnp.float32)
        column = jnp.transpose(jnp.broadcast_to(row, (128, count)))
        hot = jnp.concatenate(
            [
                jnp.where(column == lane + float(at), 1.0, 0.0).astype(jnp.bfloat16)
                for at in range(0, span, 128)
            ],
            axis=1,
        )
        packed[k] = jnp.dot(hot, feat[...], preferred_element_type=jnp.float32).astype(
            jnp.bfloat16
        )

    pack(2)
    pl.semaphore_wait(barrier, sum(there.astype(jnp.int32) for there, _ in near))
    for k in (2, 3, 1, 0):
        there, target = near[k]
        if k != 2:
            pack(k)

        @pl.when(there)
        def _():
            halo_copy(packed, halo_ref, send, recv, k, target).start()

        @pl.when(jnp.logical_not(there))
        def _():
            halo_ref[k] = jnp.zeros(halo_ref.shape[1:], halo_ref.dtype)

    table_ref[...] = jnp.zeros_like(table_ref)
    for i, line in enumerate(
        tables(row_ref, col_ref, pads, count_ref[0], row_blocks, col_blocks)
    ):
        table_ref[pl.ds(i, 1), :] = line.astype(jnp.int32)

    for k in range(4):
        there, target = near[k]

        @pl.when(there)
        def _():
            halo_copy(packed, halo_ref, send, recv, k, target).wait_send()
            halo_copy(packed, halo_ref, send, recv, k ^ 1, target).wait_recv()


def layer_kernel(
    step,
    rows,
    cols,
    live,
    nodes_live,
    feat_hbm,
    halo_hbm,
    adj_hbm,
    grad_hbm,
    w_ref,
    b_ref,
    out_hbm,
    back_hbm,
    wg_ref,
    bg_ref,
    ext,
    adj,
    grad,
    acc,
    back,
    out,
    wsum,
    bsum,
    sem,
    out_sem,
    back_sem,
):
    row_blocks, side, width = feat_hbm.shape
    halo_blocks = halo_hbm.shape[0]
    count = live[0]
    keep_to = nodes_live[0]
    loads = [
        pltpu.make_async_copy(feat_hbm, ext.at[pl.ds(0, row_blocks)], sem.at[0]),
        pltpu.make_async_copy(halo_hbm, ext.at[pl.ds(row_blocks, halo_blocks)], sem.at[1]),
        pltpu.make_async_copy(adj_hbm, adj, sem.at[2]),
        pltpu.make_async_copy(grad_hbm, grad, sem.at[3]),
    ]
    for load in loads[:3]:
        load.start()

    def clear(i, carry):
        acc[i] = jnp.zeros((side, width), jnp.float32)
        return carry

    lax.fori_loop(0, row_blocks + 1, clear, 0)
    wsum[...] = jnp.zeros_like(wsum)
    bsum[...] = jnp.zeros_like(bsum)
    for load in loads[:3]:
        load.wait()
    loads[3].start()

    def kept(block, blocks=1):
        at = lax.broadcasted_iota(jnp.int32, (blocks * side, width), 0)
        return at < keep_to - block * side

    def mask(i, carry):
        ext[i] = jnp.where(kept(i), ext[i].astype(jnp.float32), 0.0).astype(ext.dtype)
        return carry

    lax.fori_loop(keep_to // side, row_blocks, mask, 0)

    unroll = 8
    trips = (count + unroll - 1) // unroll

    def forward(t, carry):
        for u in range(unroll):
            b = t * unroll + u
            to = jnp.where(b < count, rows[b], row_blocks)
            acc[to] += jnp.dot(adj[b], ext[cols[b]], preferred_element_type=jnp.float32)
        return carry

    lax.fori_loop(0, trips, forward, 0)
    loads[3].wait()

    def put(i):
        return pltpu.make_async_copy(
            out.at[pl.ds(i * step, step)], out_hbm.at[pl.ds(i * step, step)], out_sem.at[i]
        )

    def put_back(i):
        return pltpu.make_async_copy(
            back.at[pl.ds(i * step, step)], back_hbm.at[pl.ds(i * step, step)], back_sem.at[i]
        )

    tall = step * side

    def into(i):
        at = pl.ds(i * step, step)
        agg = acc[at].reshape(tall, width).astype(jnp.bfloat16)
        return agg, jnp.dot(agg, w_ref[...], preferred_element_type=jnp.float32)

    def middle(i, pre):
        at = pl.ds(i * step, step)
        pre = pre + b_ref[...]
        keep = kept(i * step, step)
        sig = 0.5 * jnp.tanh(0.5 * pre) + 0.5
        act = pre * sig
        out[at] = jnp.where(keep, act, 0.0).astype(jnp.bfloat16).reshape(step, side, width)
        put(i).start()
        g = grad[at].reshape(tall, width).astype(jnp.float32)
        dpre = jnp.where(keep, g * (sig + act * (1.0 - sig)), 0.0).astype(jnp.bfloat16)
        bsum[...] += jnp.sum(dpre.astype(jnp.float32).reshape(tall // 8, 8, width), 0)
        return dpre

    def after(i, agg, dpre):
        wsum[...] += lax.dot_general(
            agg, dpre, (((0,), (0,)), ((), ())), preferred_element_type=jnp.float32
        )
        back[pl.ds(i * step, step)] = (
            lax.dot_general(
                dpre, w_ref[...], (((1,), (1,)), ((), ())), preferred_element_type=jnp.float32
            )
            .astype(jnp.bfloat16)
            .reshape(step, side, width)
        )
        put_back(i).start()

    group = 4

    def dense(t, carry):
        now = into(t * group)
        for u in range(group):
            i = t * group + u
            later = into(i + 1) if u + 1 < group else None
            dpre = middle(i, now[1])
            after(i, now[0], dpre)
            now = later
        return carry

    lax.fori_loop(0, row_blocks // step // group, dense, 0)
    wg_ref[...] = wsum[...].astype(wg_ref.dtype)
    bg_ref[...] = jnp.sum(bsum[...], 0, keepdims=True)

    def drain(i, carry):
        put(i).wait()
        put_back(i).wait()
        return carry

    lax.fori_loop(0, row_blocks // step, drain, 0)


def back_kernel(
    n_wide,
    n_narrow,
    scale,
    table,
    nodes_live,
    idx_ref,
    wg_ref,
    bg_ref,
    adj_hbm,
    back_hbm,
    grad_hbm,
    wout_ref,
    bout_ref,
    grad_ref,
    grad_sem,
    adj,
    back,
    run,
    ret,
    incoming,
    rs_wide,
    rs_narrow,
    part,
    ag_narrow,
    ag_wide,
    b_wide,
    b_mid,
    b_narrow,
    load,
    send,
    recv,
    send_w,
    recv_w,
    send_n,
    recv_n,
    send_gn,
    recv_gn,
    send_gw,
    recv_gw,
    send_bw,
    recv_bw,
    send_bn,
    recv_bn,
):
    w = lax.axis_index("wide")
    n = lax.axis_index("narrow")
    slab = wg_ref.shape[1]
    part_width = rs_narrow.shape[2]
    row_blocks, side, width = back.shape
    slots = adj.shape[0]
    loads = [
        pltpu.make_async_copy(back_hbm, back, load.at[0]),
        pltpu.make_async_copy(adj_hbm, adj, load.at[1]),
    ]
    for fetch in loads:
        fetch.start()

    def wide_peer(d):
        return (lax.rem(w + d, n_wide), n)

    def narrow_peer(d):
        return (w, lax.rem(n + d, n_narrow))

    peers = [wide_peer(d) for d in range(1, n_wide)] + [
        narrow_peer(d) for d in range(1, n_narrow)
    ]
    barrier = pltpu.get_barrier_semaphore()
    for peer in peers:
        pl.semaphore_signal(barrier, inc=1, device_id=peer, device_id_type=MESH)
    pl.semaphore_wait(barrier, len(peers))

    def remote(src, dst, s, r, peer):
        return pltpu.make_async_remote_copy(
            src_ref=src, dst_ref=dst, send_sem=s, recv_sem=r, device_id=peer, device_id_type=MESH
        )

    pending = []
    near = neighbours(n_wide, n_narrow)

    first = []
    for d in range(1, n_wide):
        peer = wide_peer(d)
        c = remote(wg_ref.at[peer[0]], rs_wide.at[d], send_w.at[d], recv_w.at[d], peer)
        c.start()
        first.append(c)
    bias_first = []
    for d in range(1, n_wide):
        c = remote(bg_ref, b_wide.at[d], send_bw.at[d], recv_bw.at[d], wide_peer(d))
        c.start()
        bias_first.append(c)
    run[0] = jnp.zeros(run.shape[1:], run.dtype)
    for fetch in loads:
        fetch.wait()
    unroll = 8

    def backward(t, carry):
        held = run[t * unroll]
        for u in range(unroll):
            k = t * unroll + u
            held = held * table[2, k].astype(jnp.float32) + lax.dot_general(
                adj[table[0, k]],
                back[table[1, k]],
                (((0,), (0,)), ((), ())),
                preferred_element_type=jnp.float32,
            )
            run[k + 1] = held
        return carry

    early = (slots - row_blocks) // unroll
    lax.fori_loop(0, early, backward, 0)
    halo_blocks = ret.shape[0] * ret.shape[1] // side
    per = ret.shape[1] // side
    for k in (2, 3, 1, 0):
        there, target = near[k]
        for j in range(per):
            ret[k, pl.ds(j * side, side), :] = run[table[3, k * per + j]].astype(ret.dtype)

        @pl.when(there)
        def _():
            halo_copy(ret, incoming, send, recv, k, target).start()

        @pl.when(jnp.logical_not(there))
        def _():
            incoming[k] = jnp.zeros(incoming.shape[1:], incoming.dtype)

    total = wg_ref[w].astype(jnp.float32)
    for c in first:
        c.wait_recv()
    for d in range(1, n_wide):
        total = total + rs_wide[d].astype(jnp.float32)
    bias = bg_ref[...]
    for c in bias_first:
        c.wait_recv()
    for d in range(1, n_wide):
        bias = bias + b_wide[d]
    b_mid[...] = bias
    for j in range(n_narrow):
        part[j] = total[:, j * part_width : (j + 1) * part_width].astype(part.dtype)
    second = []
    for d in range(1, n_narrow):
        peer = narrow_peer(d)
        c = remote(part.at[peer[1]], rs_narrow.at[d], send_n.at[d], recv_n.at[d], peer)
        c.start()
        second.append(c)
    for d in range(1, n_narrow):
        c = remote(b_mid, b_narrow.at[d], send_bn.at[d], recv_bn.at[d], narrow_peer(d))
        c.start()
        bias_first.append(c)
        second.append(c)
    lax.fori_loop(early, slots // unroll, backward, 0)
    piece = part[n].astype(jnp.float32)
    for c in second:
        c.wait_recv()
    for d in range(1, n_narrow):
        piece = piece + rs_narrow[d].astype(jnp.float32)
        bias = bias + b_narrow[d]
    bout_ref[...] = bias * scale
    ag_narrow[n] = (piece * scale).astype(ag_narrow.dtype)
    third = []
    for d in range(1, n_narrow):
        c = remote(
            ag_narrow.at[n], ag_narrow.at[n], send_gn.at[d], recv_gn.at[d], narrow_peer(d)
        )
        c.start()
        third.append(c)
    chunk = grad_ref.shape[1]
    across = chunk // side
    keep_to = nodes_live[0]

    def own(i):
        return jnp.concatenate(
            [run[table[3, halo_blocks + i * across + j]] for j in range(across)], 0
        )

    def leave(i):
        return pltpu.make_async_copy(grad_ref.at[i], grad_hbm.at[i], grad_sem.at[i])

    def finish(i, full):
        row = lax.broadcasted_iota(jnp.int32, full.shape, 0) + i * chunk
        grad_ref[i] = jnp.where(row < keep_to, full, 0.0).astype(grad_ref.dtype)
        leave(i).start()

    low_chunks = row_blocks // across // 2

    def high(i, carry):
        finish(i, own(i))
        return carry

    lax.fori_loop(low_chunks, row_blocks // across, high, 0)
    for c in third:
        c.wait_recv()
    fourth = []
    for d in range(1, n_wide):
        c = remote(ag_narrow, ag_wide.at[w], send_gw.at[d], recv_gw.at[d], wide_peer(d))
        c.start()
        fourth.append(c)
    ag_wide[w] = ag_narrow[...]

    for k in range(4):
        there, target = near[k]

        @pl.when(there)
        def _():
            halo_copy(ret, incoming, send, recv, k, target).wait_send()
            halo_copy(ret, incoming, send, recv, k ^ 1, target).wait_recv()

    merged = incoming[...].reshape(-1, width)
    idx = jnp.concatenate([idx_ref[0, k : k + 1, :] for k in range(4)], 1)

    def scatter(i, carry):
        at = lax.broadcasted_iota(jnp.int32, (chunk, idx.shape[1]), 0) + i * chunk
        hot = jnp.where(at == idx, 1.0, 0.0).astype(jnp.bfloat16)
        finish(i, own(i) + jnp.dot(hot, merged, preferred_element_type=jnp.float32))
        return carry

    lax.fori_loop(0, low_chunks, scatter, 0)
    for c in fourth:
        c.wait_recv()
    for i in range(n_wide):
        for j in range(n_narrow):
            wout_ref[pl.ds(i * slab, slab), pl.ds(j * part_width, part_width)] = ag_wide[
                i, j
            ].astype(jnp.float32)
    def drain(i, carry):
        leave(i).wait()
        return carry

    lax.fori_loop(0, row_blocks // across, drain, 0)
    for c in first + bias_first + second[: n_narrow - 1] + third + fourth:
        c.wait_send()


def hand_on(grad_in, w_in, b_in, grad_out, w_out, b_out, grad, wg, bg, take, give):
    pieces = grad.shape[0]
    hops = [(grad_in.at[i], grad.at[i], grad_out.at[i]) for i in range(pieces)]
    hops += [(w_in, wg, w_out), (b_in, bg, b_out)]
    ins = [pltpu.make_async_copy(a, b, take.at[i]) for i, (a, b, _) in enumerate(hops)]
    outs = [pltpu.make_async_copy(b, c, give.at[i]) for i, (_, b, c) in enumerate(hops)]
    for c in ins:
        c.start()
    for c, d in zip(ins, outs):
        c.wait()
        d.start()
    for d in outs:
        d.wait()


def local(
    n_wide,
    n_narrow,
    features,
    adjacency,
    block_rows,
    block_cols,
    block_count,
    node_count,
    halo_index,
    weight,
    bias,
    out_grad,
):
    nodes, width = features.shape
    slots, side, _ = adjacency.shape
    row_blocks = nodes // side
    sides, halo = halo_index.shape[1:]
    halo_blocks = sides * halo // side
    col_blocks = row_blocks + halo_blocks
    bf, f32 = jnp.bfloat16, jnp.float32
    vm = pl.BlockSpec(memory_space=pltpu.VMEM)
    sm = pl.BlockSpec(memory_space=pltpu.SMEM)
    hb = pl.BlockSpec(memory_space=ANY)
    dma = pltpu.SemaphoreType.DMA

    lanes = -(-slots // 128) * 128
    halos, table = pl.pallas_call(
        functools.partial(gather_kernel, n_wide, n_narrow, row_blocks, col_blocks),
        name="halo_out",
        out_shape=(
            jax.ShapeDtypeStruct((sides, halo, width), bf),
            jax.ShapeDtypeStruct((8, lanes), jnp.int32),
        ),
        in_specs=[vm, vm, vm, sm, hb],
        out_specs=(vm, vm),
        scratch_shapes=[
            pltpu.VMEM((8, lanes), jnp.int32),
            pltpu.VMEM((nodes // 2, width), bf),
            pltpu.VMEM((sides, halo, width), bf),
            dma,
            dma((sides,)),
            dma((sides,)),
        ],
        compiler_params=pltpu.CompilerParams(
            collective_id=0, has_side_effects=True, vmem_limit_bytes=VMEM_LIMIT
        ),
    )(
        halo_index,
        block_rows,
        block_cols,
        block_count,
        features,
    )

    step = 2
    blocked = (row_blocks, side, width)
    out, back, wg, bg = pl.pallas_call(
        functools.partial(layer_kernel, step),
        name="layer",
        out_shape=(
            jax.ShapeDtypeStruct(blocked, bf),
            jax.ShapeDtypeStruct(blocked, bf),
            jax.ShapeDtypeStruct((width, width), bf),
            jax.ShapeDtypeStruct((1, width), f32),
        ),
        in_specs=[sm, sm, sm, sm, hb, hb, hb, hb, vm, vm],
        out_specs=(hb, hb, vm, vm),
        scratch_shapes=[
            pltpu.VMEM((col_blocks, side, width), bf),
            pltpu.VMEM((slots, side, side), bf),
            pltpu.VMEM(blocked, bf),
            pltpu.VMEM((row_blocks + 1, side, width), f32),
            pltpu.VMEM(blocked, bf),
            pltpu.VMEM(blocked, bf),
            pltpu.VMEM((width, width), f32),
            pltpu.VMEM((8, width), f32),
            dma((4,)),
            dma((row_blocks // step,)),
            dma((row_blocks // step,)),
        ],
        compiler_params=pltpu.CompilerParams(vmem_limit_bytes=VMEM_LIMIT),
    )(
        block_rows[0],
        block_cols[0],
        block_count,
        node_count,
        features.reshape(blocked),
        halos.reshape(halo_blocks, side, width),
        adjacency,
        out_grad.reshape(blocked),
        weight,
        bias.reshape(1, width),
    )

    slab = width // n_wide
    part_width = width // n_narrow
    scale = 1.0 / math.sqrt(nodes * n_wide * n_narrow)
    chunk = 2 * side
    input_grad, wout, bout = pl.pallas_call(
        functools.partial(back_kernel, n_wide, n_narrow, scale),
        name="back",
        out_shape=(
            jax.ShapeDtypeStruct((nodes // chunk, chunk, width), bf),
            jax.ShapeDtypeStruct((width, width), f32),
            jax.ShapeDtypeStruct((1, width), f32),
        ),
        in_specs=[sm, sm, vm, vm, vm, hb, hb],
        out_specs=(hb, vm, vm),
        scratch_shapes=[
            pltpu.VMEM((nodes // chunk, chunk, width), bf),
            dma((nodes // chunk,)),
            pltpu.VMEM((slots, side, side), bf),
            pltpu.VMEM(blocked, bf),
            pltpu.VMEM((slots + 1, side, width), f32),
            pltpu.VMEM((sides, halo, width), bf),
            pltpu.VMEM((sides, halo, width), bf),
            pltpu.VMEM((n_wide, slab, width), bf),
            pltpu.VMEM((n_narrow, slab, part_width), bf),
            pltpu.VMEM((n_narrow, slab, part_width), bf),
            pltpu.VMEM((n_narrow, slab, part_width), bf),
            pltpu.VMEM((n_wide, n_narrow, slab, part_width), bf),
            pltpu.VMEM((n_wide, 1, width), f32),
            pltpu.VMEM((1, width), f32),
            pltpu.VMEM((n_narrow, 1, width), f32),
            dma((2,)),
            dma((sides,)),
            dma((sides,)),
        ]
        + [dma((n_wide,))] * 2
        + [dma((n_narrow,))] * 4
        + [dma((n_wide,))] * 4
        + [dma((n_narrow,))] * 2,
        compiler_params=pltpu.CompilerParams(
            collective_id=1, has_side_effects=True, vmem_limit_bytes=VMEM_LIMIT
        ),
    )(
        table,
        node_count,
        halo_index,
        wg.reshape(n_wide, slab, width),
        bg,
        adjacency,
        back,
    )
    pieces = 8
    input_grad, wout, bout = pl.pallas_call(
        hand_on,
        name="hand_on",
        out_shape=(
            jax.ShapeDtypeStruct((pieces, nodes // pieces, width), bf),
            jax.ShapeDtypeStruct((width, width), f32),
            jax.ShapeDtypeStruct((1, width), f32),
        ),
        in_specs=[hb, hb, hb],
        out_specs=(hb, hb, hb),
        scratch_shapes=[
            pltpu.VMEM((pieces, nodes // pieces, width), bf),
            pltpu.VMEM((width, width), f32),
            pltpu.VMEM((1, width), f32),
            dma((pieces + 2,)),
            dma((pieces + 2,)),
        ],
        compiler_params=pltpu.CompilerParams(vmem_limit_bytes=VMEM_LIMIT),
    )(input_grad.reshape(pieces, nodes // pieces, width), wout, bout)
    return out.reshape(nodes, width), input_grad.reshape(nodes, width), wout, bout.reshape(width)


def solution(mesh):
    both = ("wide", "narrow")
    placed = (
        P(both, None),
        P(both, None, None),
        P(both, None),
        P(both, None),
        P(both),
        P(both),
        P(both, None, None),
        P(),
        P(),
        P(both, None),
    )
    return jax.shard_map(
        functools.partial(local, mesh.shape["wide"], mesh.shape["narrow"]),
        mesh=mesh,
        in_specs=placed,
        out_specs=(P(both, None), P(both, None), P(), P()),
        check_vma=False,
    )
```

```python
import functools
import math

import jax
import jax.numpy as jnp
from jax import lax
from jax.experimental import pallas as pl
from jax.experimental.pallas import tpu as pltpu
from jax.sharding import PartitionSpec as P

MESH = pl.DeviceIdType.MESH
ANY = pl.ANY
VMEM_LIMIT = 60 * 1024 * 1024


def neighbours(n_wide, n_narrow):
    w = lax.axis_index("wide")
    n = lax.axis_index("narrow")
    return (
        (w > 0, (w - 1, n)),
        (w < n_wide - 1, (w + 1, n)),
        (n > 0, (w, n - 1)),
        (n < n_narrow - 1, (w, n + 1)),
    )


def halo_copy(src, dst, send, recv, k, target):
    return pltpu.make_async_remote_copy(
        src_ref=src.at[k],
        dst_ref=dst.at[k ^ 1],
        send_sem=send.at[k],
        recv_sem=recv.at[k ^ 1],
        device_id=target,
        device_id_type=MESH,
    )


def tables(row_ref, col_ref, pads, count, row_blocks, col_blocks):
    lanes = pads.shape[1]
    slots = row_ref.shape[1]
    f32 = jnp.float32
    pads[...] = jnp.zeros_like(pads)
    pads[0:1, 0:slots] = row_ref[...]
    pads[1:2, 0:slots] = col_ref[...]
    lane = lax.broadcasted_iota(jnp.int32, (lanes, lanes), 1).astype(f32)
    sub = lax.broadcasted_iota(jnp.int32, (lanes, lanes), 0).astype(f32)

    def spread(x):
        return jnp.broadcast_to(x.astype(f32), (lanes, lanes))

    halo_blocks = col_blocks - row_blocks
    col = spread(pads[1:2, :])
    place = jnp.where(col >= row_blocks, col - row_blocks, col + halo_blocks)
    place = jnp.where(lane < count.astype(f32), place, float(col_blocks))
    place_t = jnp.transpose(place)
    row_t = jnp.transpose(spread(pads[0:1, :]))
    same = place == place_t
    ahead = lane < sub
    one = lambda m: jnp.where(m, 1.0, 0.0)
    rank = jnp.sum(one((place < place_t) | (same & ahead)), 1, keepdims=True)
    twin = jnp.minimum(jnp.sum(one(same & ahead), 1, keepdims=True), 1.0)
    hot = one(jnp.broadcast_to(rank, (lanes, lanes)) == lane)
    pick = lambda x: jnp.sum(hot * x, 0, keepdims=True)
    ends = jnp.sum(one(place_t <= lane), 0, keepdims=True)
    keep = pick(jnp.broadcast_to(twin, (lanes, lanes)))
    return pick(sub), pick(row_t), keep, ends


def gather_kernel(
    n_wide,
    n_narrow,
    row_blocks,
    col_blocks,
    idx_ref,
    row_ref,
    col_ref,
    count_ref,
    feat_hbm,
    halo_ref,
    table_ref,
    pads,
    feat,
    packed,
    load,
    send,
    recv,
):
    count = idx_ref.shape[2]
    span = feat.shape[0]
    fetch = pltpu.make_async_copy(feat_hbm.at[pl.ds(0, span)], feat, load)
    fetch.start()
    near = neighbours(n_wide, n_narrow)
    barrier = pltpu.get_barrier_semaphore()
    for there, target in near:

        @pl.when(there)
        def _():
            pl.semaphore_signal(barrier, inc=1, device_id=target, device_id_type=MESH)

    fetch.wait()
    lane = lax.broadcasted_iota(jnp.int32, (count, 128), 1).astype(jnp.float32)

    def pack(k):
        row = idx_ref[0, pl.ds(k, 1), :].astype(jnp.float32)
        column = jnp.transpose(jnp.broadcast_to(row, (128, count)))
        hot = jnp.concatenate(
            [
                jnp.where(column == lane + float(at), 1.0, 0.0).astype(jnp.bfloat16)
                for at in range(0, span, 128)
            ],
            axis=1,
        )
        packed[k] = jnp.dot(hot, feat[...], preferred_element_type=jnp.float32).astype(
            jnp.bfloat16
        )

    pack(2)
    pl.semaphore_wait(barrier, sum(there.astype(jnp.int32) for there, _ in near))
    for k in (2, 3, 1, 0):
        there, target = near[k]
        if k != 2:
            pack(k)

        @pl.when(there)
        def _():
            halo_copy(packed, halo_ref, send, recv, k, target).start()

        @pl.when(jnp.logical_not(there))
        def _():
            halo_ref[k] = jnp.zeros(halo_ref.shape[1:], halo_ref.dtype)

    table_ref[...] = jnp.zeros_like(table_ref)
    for i, line in enumerate(
        tables(row_ref, col_ref, pads, count_ref[0], row_blocks, col_blocks)
    ):
        table_ref[pl.ds(i, 1), :] = line.astype(jnp.int32)

    for k in range(4):
        there, target = near[k]

        @pl.when(there)
        def _():
            halo_copy(packed, halo_ref, send, recv, k, target).wait_send()
            halo_copy(packed, halo_ref, send, recv, k ^ 1, target).wait_recv()


def layer_kernel(
    step,
    rows,
    cols,
    live,
    nodes_live,
    feat_hbm,
    halo_hbm,
    adj_hbm,
    grad_hbm,
    w_ref,
    b_ref,
    out_hbm,
    back_hbm,
    wg_ref,
    bg_ref,
    ext,
    adj,
    grad,
    acc,
    back,
    out,
    wsum,
    bsum,
    sem,
    out_sem,
    back_sem,
):
    row_blocks, side, width = feat_hbm.shape
    halo_blocks = halo_hbm.shape[0]
    count = live[0]
    keep_to = nodes_live[0]
    loads = [
        pltpu.make_async_copy(feat_hbm, ext.at[pl.ds(0, row_blocks)], sem.at[0]),
        pltpu.make_async_copy(halo_hbm, ext.at[pl.ds(row_blocks, halo_blocks)], sem.at[1]),
        pltpu.make_async_copy(adj_hbm, adj, sem.at[2]),
        pltpu.make_async_copy(grad_hbm, grad, sem.at[3]),
    ]
    for load in loads[:3]:
        load.start()

    def clear(i, carry):
        acc[i] = jnp.zeros((side, width), jnp.float32)
        return carry

    lax.fori_loop(0, row_blocks + 1, clear, 0)
    wsum[...] = jnp.zeros_like(wsum)
    bsum[...] = jnp.zeros_like(bsum)
    for load in loads[:3]:
        load.wait()
    loads[3].start()

    def kept(block, blocks=1):
        at = lax.broadcasted_iota(jnp.int32, (blocks * side, width), 0)
        return at < keep_to - block * side

    def mask(i, carry):
        ext[i] = jnp.where(kept(i), ext[i].astype(jnp.float32), 0.0).astype(ext.dtype)
        return carry

    lax.fori_loop(keep_to // side, row_blocks, mask, 0)

    unroll = 16
    trips = (count + unroll - 1) // unroll

    def forward(t, carry):
        for u in range(unroll):
            b = t * unroll + u
            to = jnp.where(b < count, rows[b], row_blocks)
            acc[to] += jnp.dot(adj[b], ext[cols[b]], preferred_element_type=jnp.float32)
        return carry

    lax.fori_loop(0, trips, forward, 0)
    loads[3].wait()

    def put(i):
        return pltpu.make_async_copy(
            out.at[pl.ds(i * step, step)], out_hbm.at[pl.ds(i * step, step)], out_sem.at[i]
        )

    def put_back(i):
        return pltpu.make_async_copy(
            back.at[pl.ds(i * step, step)], back_hbm.at[pl.ds(i * step, step)], back_sem.at[i]
        )

    tall = step * side

    def into(i):
        at = pl.ds(i * step, step)
        agg = acc[at].reshape(tall, width).astype(jnp.bfloat16)
        return agg, jnp.dot(agg, w_ref[...], preferred_element_type=jnp.float32)

    def middle(i, pre):
        at = pl.ds(i * step, step)
        pre = pre + b_ref[...]
        keep = kept(i * step, step)
        sig = 0.5 * jnp.tanh(0.5 * pre) + 0.5
        act = pre * sig
        out[at] = jnp.where(keep, act, 0.0).astype(jnp.bfloat16).reshape(step, side, width)
        put(i).start()
        g = grad[at].reshape(tall, width).astype(jnp.float32)
        dpre = jnp.where(keep, g * (sig + act * (1.0 - sig)), 0.0).astype(jnp.bfloat16)
        bsum[...] += jnp.sum(dpre.astype(jnp.float32).reshape(tall // 8, 8, width), 0)
        return dpre

    def after(i, agg, dpre):
        wsum[...] += lax.dot_general(
            agg, dpre, (((0,), (0,)), ((), ())), preferred_element_type=jnp.float32
        )
        back[pl.ds(i * step, step)] = (
            lax.dot_general(
                dpre, w_ref[...], (((1,), (1,)), ((), ())), preferred_element_type=jnp.float32
            )
            .astype(jnp.bfloat16)
            .reshape(step, side, width)
        )
        put_back(i).start()

    group = 8

    def dense(t, carry):
        now = into(t * group)
        for u in range(group):
            i = t * group + u
            later = into(i + 1) if u + 1 < group else None
            dpre = middle(i, now[1])
            after(i, now[0], dpre)
            now = later
        return carry

    lax.fori_loop(0, row_blocks // step // group, dense, 0)
    wg_ref[...] = wsum[...].astype(wg_ref.dtype)
    bg_ref[...] = jnp.sum(bsum[...], 0, keepdims=True)

    def drain(i, carry):
        put(i).wait()
        put_back(i).wait()
        return carry

    lax.fori_loop(0, row_blocks // step, drain, 0)


def back_kernel(
    n_wide,
    n_narrow,
    scale,
    table,
    nodes_live,
    idx_ref,
    wg_ref,
    bg_ref,
    adj_hbm,
    back_hbm,
    grad_hbm,
    wout_ref,
    bout_ref,
    grad_ref,
    grad_sem,
    adj,
    back,
    run,
    ret,
    incoming,
    rs_wide,
    rs_narrow,
    part,
    ag_narrow,
    ag_wide,
    b_wide,
    b_mid,
    b_narrow,
    load,
    send,
    recv,
    send_w,
    recv_w,
    send_n,
    recv_n,
    send_gn,
    recv_gn,
    send_gw,
    recv_gw,
    send_bw,
    recv_bw,
    send_bn,
    recv_bn,
):
    w = lax.axis_index("wide")
    n = lax.axis_index("narrow")
    slab = wg_ref.shape[1]
    part_width = rs_narrow.shape[2]
    row_blocks, side, width = back.shape
    slots = adj.shape[0]
    loads = [
        pltpu.make_async_copy(back_hbm, back, load.at[0]),
        pltpu.make_async_copy(adj_hbm, adj, load.at[1]),
    ]
    for fetch in loads:
        fetch.start()

    def wide_peer(d):
        return (lax.rem(w + d, n_wide), n)

    def narrow_peer(d):
        return (w, lax.rem(n + d, n_narrow))

    peers = [wide_peer(d) for d in range(1, n_wide)] + [
        narrow_peer(d) for d in range(1, n_narrow)
    ]
    barrier = pltpu.get_barrier_semaphore()
    for peer in peers:
        pl.semaphore_signal(barrier, inc=1, device_id=peer, device_id_type=MESH)
    pl.semaphore_wait(barrier, len(peers))

    def remote(src, dst, s, r, peer):
        return pltpu.make_async_remote_copy(
            src_ref=src, dst_ref=dst, send_sem=s, recv_sem=r, device_id=peer, device_id_type=MESH
        )

    pending = []
    near = neighbours(n_wide, n_narrow)

    first = []
    for d in range(1, n_wide):
        peer = wide_peer(d)
        c = remote(wg_ref.at[peer[0]], rs_wide.at[d], send_w.at[d], recv_w.at[d], peer)
        c.start()
        first.append(c)
    bias_first = []
    for d in range(1, n_wide):
        c = remote(bg_ref, b_wide.at[d], send_bw.at[d], recv_bw.at[d], wide_peer(d))
        c.start()
        bias_first.append(c)
    run[0] = jnp.zeros(run.shape[1:], run.dtype)
    for fetch in loads:
        fetch.wait()
    unroll = 16

    def backward(t, carry):
        held = run[t * unroll]
        for u in range(unroll):
            k = t * unroll + u
            held = held * table[2, k].astype(jnp.float32) + lax.dot_general(
                adj[table[0, k]],
                back[table[1, k]],
                (((0,), (0,)), ((), ())),
                preferred_element_type=jnp.float32,
            )
            run[k + 1] = held
        return carry

    early = (slots - row_blocks) // unroll
    lax.fori_loop(0, early, backward, 0)
    halo_blocks = ret.shape[0] * ret.shape[1] // side
    per = ret.shape[1] // side
    for k in (2, 3, 1, 0):
        there, target = near[k]
        for j in range(per):
            ret[k, pl.ds(j * side, side), :] = run[table[3, k * per + j]].astype(ret.dtype)

        @pl.when(there)
        def _():
            halo_copy(ret, incoming, send, recv, k, target).start()

        @pl.when(jnp.logical_not(there))
        def _():
            incoming[k] = jnp.zeros(incoming.shape[1:], incoming.dtype)

    total = wg_ref[w].astype(jnp.float32)
    for c in first:
        c.wait_recv()
    for d in range(1, n_wide):
        total = total + rs_wide[d].astype(jnp.float32)
    bias = bg_ref[...]
    for c in bias_first:
        c.wait_recv()
    for d in range(1, n_wide):
        bias = bias + b_wide[d]
    b_mid[...] = bias
    for j in range(n_narrow):
        part[j] = total[:, j * part_width : (j + 1) * part_width].astype(part.dtype)
    second = []
    for d in range(1, n_narrow):
        peer = narrow_peer(d)
        c = remote(part.at[peer[1]], rs_narrow.at[d], send_n.at[d], recv_n.at[d], peer)
        c.start()
        second.append(c)
    for d in range(1, n_narrow):
        c = remote(b_mid, b_narrow.at[d], send_bn.at[d], recv_bn.at[d], narrow_peer(d))
        c.start()
        bias_first.append(c)
        second.append(c)
    lax.fori_loop(early, slots // unroll, backward, 0)
    piece = part[n].astype(jnp.float32)
    for c in second:
        c.wait_recv()
    for d in range(1, n_narrow):
        piece = piece + rs_narrow[d].astype(jnp.float32)
        bias = bias + b_narrow[d]
    bout_ref[...] = bias * scale
    ag_narrow[n] = (piece * scale).astype(ag_narrow.dtype)
    third = []
    for d in range(1, n_narrow):
        c = remote(
            ag_narrow.at[n], ag_narrow.at[n], send_gn.at[d], recv_gn.at[d], narrow_peer(d)
        )
        c.start()
        third.append(c)
    chunk = grad_ref.shape[1]
    across = chunk // side
    keep_to = nodes_live[0]

    def own(i):
        return jnp.concatenate(
            [run[table[3, halo_blocks + i * across + j]] for j in range(across)], 0
        )

    def leave(i):
        return pltpu.make_async_copy(grad_ref.at[i], grad_hbm.at[i], grad_sem.at[i])

    def finish(i, full):
        row = lax.broadcasted_iota(jnp.int32, full.shape, 0) + i * chunk
        grad_ref[i] = jnp.where(row < keep_to, full, 0.0).astype(grad_ref.dtype)
        leave(i).start()

    low_chunks = row_blocks // across // 2

    def high(i, carry):
        finish(i, own(i))
        return carry

    lax.fori_loop(low_chunks, row_blocks // across, high, 0)
    for c in third:
        c.wait_recv()
    fourth = []
    for d in range(1, n_wide):
        c = remote(ag_narrow, ag_wide.at[w], send_gw.at[d], recv_gw.at[d], wide_peer(d))
        c.start()
        fourth.append(c)
    ag_wide[w] = ag_narrow[...]

    for k in range(4):
        there, target = near[k]

        @pl.when(there)
        def _():
            halo_copy(ret, incoming, send, recv, k, target).wait_send()
            halo_copy(ret, incoming, send, recv, k ^ 1, target).wait_recv()

    merged = incoming[...].reshape(-1, width)
    idx = jnp.concatenate([idx_ref[0, k : k + 1, :] for k in range(4)], 1)

    def scatter(i, carry):
        at = lax.broadcasted_iota(jnp.int32, (chunk, idx.shape[1]), 0) + i * chunk
        hot = jnp.where(at == idx, 1.0, 0.0).astype(jnp.bfloat16)
        finish(i, own(i) + jnp.dot(hot, merged, preferred_element_type=jnp.float32))
        return carry

    lax.fori_loop(0, low_chunks, scatter, 0)
    for c in fourth:
        c.wait_recv()
    for i in range(n_wide):
        for j in range(n_narrow):
            wout_ref[pl.ds(i * slab, slab), pl.ds(j * part_width, part_width)] = ag_wide[
                i, j
            ].astype(jnp.float32)
    def drain(i, carry):
        leave(i).wait()
        return carry

    lax.fori_loop(0, row_blocks // across, drain, 0)
    for c in first + bias_first + second[: n_narrow - 1] + third + fourth:
        c.wait_send()


def hand_on(grad_in, w_in, b_in, grad_out, w_out, b_out, grad, wg, bg, take, give):
    pieces = grad.shape[0]
    hops = [(grad_in.at[i], grad.at[i], grad_out.at[i]) for i in range(pieces)]
    hops += [(w_in, wg, w_out), (b_in, bg, b_out)]
    ins = [pltpu.make_async_copy(a, b, take.at[i]) for i, (a, b, _) in enumerate(hops)]
    outs = [pltpu.make_async_copy(b, c, give.at[i]) for i, (_, b, c) in enumerate(hops)]
    for c in ins:
        c.start()
    for c, d in zip(ins, outs):
        c.wait()
        d.start()
    for d in outs:
        d.wait()


def local(
    n_wide,
    n_narrow,
    features,
    adjacency,
    block_rows,
    block_cols,
    block_count,
    node_count,
    halo_index,
    weight,
    bias,
    out_grad,
):
    nodes, width = features.shape
    slots, side, _ = adjacency.shape
    row_blocks = nodes // side
    sides, halo = halo_index.shape[1:]
    halo_blocks = sides * halo // side
    col_blocks = row_blocks + halo_blocks
    bf, f32 = jnp.bfloat16, jnp.float32
    vm = pl.BlockSpec(memory_space=pltpu.VMEM)
    sm = pl.BlockSpec(memory_space=pltpu.SMEM)
    hb = pl.BlockSpec(memory_space=ANY)
    dma = pltpu.SemaphoreType.DMA

    lanes = -(-slots // 128) * 128
    halos, table = pl.pallas_call(
        functools.partial(gather_kernel, n_wide, n_narrow, row_blocks, col_blocks),
        name="halo_out",
        out_shape=(
            jax.ShapeDtypeStruct((sides, halo, width), bf),
            jax.ShapeDtypeStruct((8, lanes), jnp.int32),
        ),
        in_specs=[vm, vm, vm, sm, hb],
        out_specs=(vm, vm),
        scratch_shapes=[
            pltpu.VMEM((8, lanes), jnp.int32),
            pltpu.VMEM((nodes // 2, width), bf),
            pltpu.VMEM((sides, halo, width), bf),
            dma,
            dma((sides,)),
            dma((sides,)),
        ],
        compiler_params=pltpu.CompilerParams(
            collective_id=0, has_side_effects=True, vmem_limit_bytes=VMEM_LIMIT
        ),
    )(
        halo_index,
        block_rows,
        block_cols,
        block_count,
        features,
    )

    step = 2
    blocked = (row_blocks, side, width)
    out, back, wg, bg = pl.pallas_call(
        functools.partial(layer_kernel, step),
        name="layer",
        out_shape=(
            jax.ShapeDtypeStruct(blocked, bf),
            jax.ShapeDtypeStruct(blocked, bf),
            jax.ShapeDtypeStruct((width, width), bf),
            jax.ShapeDtypeStruct((1, width), f32),
        ),
        in_specs=[sm, sm, sm, sm, hb, hb, hb, hb, vm, vm],
        out_specs=(hb, hb, vm, vm),
        scratch_shapes=[
            pltpu.VMEM((col_blocks, side, width), bf),
            pltpu.VMEM((slots, side, side), bf),
            pltpu.VMEM(blocked, bf),
            pltpu.VMEM((row_blocks + 1, side, width), f32),
            pltpu.VMEM(blocked, bf),
            pltpu.VMEM(blocked, bf),
            pltpu.VMEM((width, width), f32),
            pltpu.VMEM((8, width), f32),
            dma((4,)),
            dma((row_blocks // step,)),
            dma((row_blocks // step,)),
        ],
        compiler_params=pltpu.CompilerParams(vmem_limit_bytes=VMEM_LIMIT),
    )(
        block_rows[0],
        block_cols[0],
        block_count,
        node_count,
        features.reshape(blocked),
        halos.reshape(halo_blocks, side, width),
        adjacency,
        out_grad.reshape(blocked),
        weight,
        bias.reshape(1, width),
    )

    slab = width // n_wide
    part_width = width // n_narrow
    scale = 1.0 / math.sqrt(nodes * n_wide * n_narrow)
    chunk = 2 * side
    input_grad, wout, bout = pl.pallas_call(
        functools.partial(back_kernel, n_wide, n_narrow, scale),
        name="back",
        out_shape=(
            jax.ShapeDtypeStruct((nodes // chunk, chunk, width), bf),
            jax.ShapeDtypeStruct((width, width), f32),
            jax.ShapeDtypeStruct((1, width), f32),
        ),
        in_specs=[sm, sm, vm, vm, vm, hb, hb],
        out_specs=(hb, vm, vm),
        scratch_shapes=[
            pltpu.VMEM((nodes // chunk, chunk, width), bf),
            dma((nodes // chunk,)),
            pltpu.VMEM((slots, side, side), bf),
            pltpu.VMEM(blocked, bf),
            pltpu.VMEM((slots + 1, side, width), f32),
            pltpu.VMEM((sides, halo, width), bf),
            pltpu.VMEM((sides, halo, width), bf),
            pltpu.VMEM((n_wide, slab, width), bf),
            pltpu.VMEM((n_narrow, slab, part_width), bf),
            pltpu.VMEM((n_narrow, slab, part_width), bf),
            pltpu.VMEM((n_narrow, slab, part_width), bf),
            pltpu.VMEM((n_wide, n_narrow, slab, part_width), bf),
            pltpu.VMEM((n_wide, 1, width), f32),
            pltpu.VMEM((1, width), f32),
            pltpu.VMEM((n_narrow, 1, width), f32),
            dma((2,)),
            dma((sides,)),
            dma((sides,)),
        ]
        + [dma((n_wide,))] * 2
        + [dma((n_narrow,))] * 4
        + [dma((n_wide,))] * 4
        + [dma((n_narrow,))] * 2,
        compiler_params=pltpu.CompilerParams(
            collective_id=1, has_side_effects=True, vmem_limit_bytes=VMEM_LIMIT
        ),
    )(
        table,
        node_count,
        halo_index,
        wg.reshape(n_wide, slab, width),
        bg,
        adjacency,
        back,
    )
    pieces = 8
    input_grad, wout, bout = pl.pallas_call(
        hand_on,
        name="hand_on",
        out_shape=(
            jax.ShapeDtypeStruct((pieces, nodes // pieces, width), bf),
            jax.ShapeDtypeStruct((width, width), f32),
            jax.ShapeDtypeStruct((1, width), f32),
        ),
        in_specs=[hb, hb, hb],
        out_specs=(hb, hb, hb),
        scratch_shapes=[
            pltpu.VMEM((pieces, nodes // pieces, width), bf),
            pltpu.VMEM((width, width), f32),
            pltpu.VMEM((1, width), f32),
            dma((pieces + 2,)),
            dma((pieces + 2,)),
        ],
        compiler_params=pltpu.CompilerParams(vmem_limit_bytes=VMEM_LIMIT),
    )(input_grad.reshape(pieces, nodes // pieces, width), wout, bout)
    return out.reshape(nodes, width), input_grad.reshape(nodes, width), wout, bout.reshape(width)


def solution(mesh):
    both = ("wide", "narrow")
    placed = (
        P(both, None),
        P(both, None, None),
        P(both, None),
        P(both, None),
        P(both),
        P(both),
        P(both, None, None),
        P(),
        P(),
        P(both, None),
    )
    return jax.shard_map(
        functools.partial(local, mesh.shape["wide"], mesh.shape["narrow"]),
        mesh=mesh,
        in_specs=placed,
        out_specs=(P(both, None), P(both, None), P(), P()),
        check_vma=False,
    )
```
